32 devices in a mesh: row: 4 (over z), col: 8 (over y, x, core).
Axes of the slice: x: 2, y: 2, z: 4, core: 2. Of those that a mesh axis runs over, the one named last changes fastest.
Arguments:
- block_cells: float32 [352, 5, 16, 256], P(('row', 'col')), may hold values from -0.6 to 1.4, as said below
- slot_blocks: int32 [32, 11], replicated, may hold values from -1 to 191, as said below
Outputs:
- new_cells: float32 [224, 5, 16, 256], P(('row', 'col'))
The draws below stay inside these ranges and needn't reach their ends.
Inputs may be any that keep to these rules, and one draw needn't show every extreme that they name: `slot_blocks`: row r * 8 + c lists the blocks held by device (r, c): block ids first, in slot order, then -1. Block b belongs to column group b // 24, and every block of column group c is held by exactly one device of that column group. Each device holds 1 to 11 blocks, the devices of a column group hold 24 blocks together, and in every column group one device holds 11 blocks and one holds 1. `block_cells`: fields 0 and 4 (density, pressure) lie in 0.7 to 1.4 and fields 1 to 3 (velocity) in -0.6 to 0.6. Slots marked -1 in slot_blocks hold values that no output depends on.
All inputs are finite; a program needn't handle non-finite values.
Results may differ from the reference program's by a relative error of at most 0.0001.
Values sent between devices are 32-bit elements; how exact they have to be, the bound alone decides.
A program may use at most 64 MiB of HBM per device.

```python
import jax
import jax.numpy as jnp
from jax import lax

B = 16
BLK_MEAN = 6
CAP = 11
OUT = 7
NBY = 24
NBLK = 192
N_ROW = 4
N_COL = 8


def draw_slot_blocks(key, part):
    row_count = N_ROW
    columns = N_COL
    per_group = BLK_MEAN * row_count
    slot_width = 2 * BLK_MEAN - 1

    def one_group(column):
        group_key = jax.random.fold_in(jax.random.fold_in(key, 17), column)
        order_key, delta_key, block_key = jax.random.split(group_key, 3)
        shuffle = jax.random.permutation(order_key, row_count)
        deltas = jax.random.randint(delta_key, (row_count // 2 - 1,), 0, BLK_MEAN).astype(jnp.int32)
        paired = jnp.stack([BLK_MEAN + deltas, BLK_MEAN - deltas], axis=1).reshape(-1)
        values = jnp.concatenate([jnp.array([slot_width, 1], jnp.int32), paired.astype(jnp.int32)])
        counts = jnp.zeros((row_count,), jnp.int32).at[shuffle].set(values)
        starts = jnp.cumsum(counts) - counts
        blocks = column * per_group + jax.random.permutation(block_key, per_group).astype(jnp.int32)
        slot_ids = jnp.arange(slot_width, dtype=jnp.int32)
        gather_at = jnp.clip(starts[:, None] + slot_ids[None, :], 0, per_group - 1)
        return jnp.where(slot_ids[None, :] < counts[:, None], blocks[gather_at], -1)
    layout = jax.vmap(one_group)(jnp.arange(columns, dtype=jnp.int32))
    return layout.transpose(1, 0, 2).reshape(row_count * columns, slot_width).astype(jnp.int32)


def draw_block_cells(key, part):
    total_slots = N_ROW * N_COL * CAP
    shape_one = (total_slots, 1, B, B * B)
    density_key, motion_key, pressure_key = jax.random.split(jax.random.fold_in(key, 29), 3)
    matter_per_volume = jax.random.uniform(density_key, shape_one, jnp.float32, 0.7, 1.4)
    velocity = jnp.clip(0.2 * jax.random.normal(motion_key, (total_slots, 3, B, B * B), jnp.float32), -0.6, 0.6)
    fluid_static_stress = jax.random.uniform(pressure_key, shape_one, jnp.float32, 0.7, 1.4)
    return jnp.concatenate([matter_per_volume, velocity, fluid_static_stress], axis=1).astype(jnp.float32)


def setup_inputs(seed: int = 0) -> dict:
    key_list = jax.random.split(jax.random.key(seed), 3)
    block_cells = draw_block_cells(jax.random.fold_in(key_list[2], 71), 0)
    slot_blocks = draw_slot_blocks(jax.random.fold_in(key_list[2], 71), 0)
    return {"block_cells": block_cells, "slot_blocks": slot_blocks}


heat_ratio = 1.4
time_step = 0.12
thermal_leading_multiplier = 0.2
thermal_power_law_index = 0.7

def rebalance_table(anchors, counts):
    row_count, columns, slot_width = anchors.shape
    slot_ids = jnp.arange(slot_width, dtype=jnp.int32)
    row_ids = jnp.arange(row_count, dtype=jnp.int32)
    for section_bit in range(row_count.bit_length() - 1):
        partner = row_ids ^ 1 << section_bit
        other_anchors = anchors[partner]
        other_counts = counts[partner]
        sending = jnp.maximum(counts - other_counts, 0) // 2
        taking = jnp.maximum(other_counts - counts, 0) // 2
        keeping = (counts - sending)[:, :, None]
        anchor_slot = other_counts[:, :, None] - taking[:, :, None] + slot_ids - keeping
        pulled = jnp.take_along_axis(other_anchors, jnp.clip(anchor_slot, 0, slot_width - 1), axis=2)
        anchors = jnp.where(slot_ids < keeping, anchors, jnp.where(slot_ids < keeping + taking[:, :, None], pulled, -1))
        counts = counts - sending + taking
    return (anchors, counts)

def to_conserved(primitive):
    matter_per_volume = primitive[0]
    velocity = primitive[1:4]
    fluid_static_stress = primitive[4]
    energy = fluid_static_stress / (heat_ratio - 1.0) + 0.5 * matter_per_volume * lax.optimization_barrier(jnp.sum(velocity * velocity, axis=0))
    return jnp.concatenate([matter_per_volume[None], matter_per_volume[None] * velocity, energy[None]], axis=0)

def to_primitive(conserved):
    matter_per_volume = conserved[0]
    velocity = conserved[1:4] / matter_per_volume
    fluid_static_stress = (heat_ratio - 1.0) * (conserved[4] - 0.5 * matter_per_volume * lax.optimization_barrier(jnp.sum(velocity * velocity, axis=0)))
    return jnp.concatenate([matter_per_volume[None], velocity, fluid_static_stress[None]], axis=0)

def cell_terms(conserved, normal):
    matter_per_volume = conserved[0]
    momentum = conserved[1:4]
    velocity = momentum / matter_per_volume
    fluid_static_stress = (heat_ratio - 1.0) * (conserved[4] - 0.5 * matter_per_volume * lax.optimization_barrier(jnp.sum(velocity * velocity, axis=0)))
    perpendicular_flow_rate = velocity[normal]
    moment_flux = momentum * perpendicular_flow_rate
    moment_flux = moment_flux.at[normal].add(fluid_static_stress)
    face_transport_amounts = jnp.concatenate([momentum[normal][None], moment_flux, ((conserved[4] + fluid_static_stress) * perpendicular_flow_rate)[None]], axis=0)
    sound_signal_rate = jnp.sqrt(heat_ratio * fluid_static_stress / matter_per_volume)
    fluid_thermal_state = fluid_static_stress / matter_per_volume
    thermal_diffusivity_factor = thermal_leading_multiplier * jnp.power(fluid_thermal_state, thermal_power_law_index)
    return (face_transport_amounts, jnp.abs(perpendicular_flow_rate) + sound_signal_rate, fluid_thermal_state, thermal_diffusivity_factor, fluid_static_stress)

def face_flux(lower_cons, lower_data, upper_cons, upper_data):
    wave_speed = jnp.maximum(lower_data[1], upper_data[1])
    face_transport_amounts = 0.5 * (lower_data[0] + upper_data[0]) - 0.5 * wave_speed[None] * (upper_cons - lower_cons)
    heat_flow = 0.5 * (lower_data[3] + upper_data[3]) * (upper_data[2] - lower_data[2])
    return face_transport_amounts.at[4].add(-heat_flow)

def wall_flux(fluid_static_stress, normal):
    nothing = jnp.zeros_like(fluid_static_stress)
    members = [nothing, nothing, nothing, nothing, nothing]
    members[normal + 1] = fluid_static_stress
    return jnp.stack(members, axis=0)

def tendency(conserved):
    changes = []
    for normal in range(2):
        axis_at = normal - 3
        cell_data = cell_terms(conserved, normal)
        ahead_data = jax.tree.map(lambda member: jnp.roll(member, -1, axis=axis_at), cell_data)
        face_transport_amounts = face_flux(conserved, cell_data, jnp.roll(conserved, -1, axis=axis_at), ahead_data)
        changes.append(face_transport_amounts - jnp.roll(face_transport_amounts, 1, axis=axis_at))
    cell_data = cell_terms(conserved, 2)
    lower_data = jax.tree.map(lambda member: member[..., :-1], cell_data)
    upper_data = jax.tree.map(lambda member: member[..., 1:], cell_data)
    interior = face_flux(conserved[..., :-1], lower_data, conserved[..., 1:], upper_data)
    fluid_static_stress = cell_data[4]
    faces = jnp.concatenate([wall_flux(fluid_static_stress[..., :1], 2), interior, wall_flux(fluid_static_stress[..., -1:], 2)], axis=-1)
    changes.append(faces[..., 1:] - faces[..., :-1])
    return -(changes[0] + changes[1] + changes[2])

def reference(block_cells, slot_blocks):
    row_count = N_ROW
    columns = N_COL
    slot_width = slot_blocks.shape[1]
    occupied = slot_blocks >= 0
    counts = lax.optimization_barrier(jnp.sum(occupied.astype(jnp.int32), axis=1)).reshape(row_count, columns)
    device_ids = jnp.arange(row_count * columns, dtype=jnp.int32)[:, None]
    anchors = jnp.where(occupied, device_ids * slot_width + jnp.arange(slot_width, dtype=jnp.int32)[None, :], -1)
    anchors = anchors.reshape(row_count, columns, slot_width)
    final_anchors, final_counts = rebalance_table(anchors, counts)
    final_anchors = final_anchors[:, :, :OUT].reshape(-1)
    every_slot = slot_blocks.reshape(-1)
    target = jnp.where(every_slot >= 0, every_slot, NBLK)
    every_block = jnp.zeros((NBLK + 1, 5, B, B * B), jnp.float32).at[target].set(block_cells)[:NBLK]
    grid_x = jnp.arange(columns, dtype=jnp.int32)[:, None]
    grid_y = jnp.arange(NBY, dtype=jnp.int32)[None, :]
    placed = (grid_x + grid_y) % columns * NBY + grid_y
    cell_grid = every_block[placed.reshape(-1)].reshape(columns, NBY, 5, B, B, B)
    cell_grid = cell_grid.transpose(2, 0, 3, 1, 4, 5).reshape(5, columns * B, NBY * B, B)
    initial = to_conserved(cell_grid)
    first_section = initial + time_step * tendency(initial)
    second_section = 0.75 * initial + 0.25 * (first_section + time_step * tendency(first_section))
    third_section = 1.0 / 3.0 * initial + 2.0 / 3.0 * (second_section + time_step * tendency(second_section))
    finished = to_primitive(third_section).reshape(5, columns, B, NBY, B, B)
    by_position = finished.transpose(1, 3, 0, 2, 4, 5).reshape(columns * NBY, 5, B, B * B)
    final_ids = jnp.where(final_anchors >= 0, every_slot[jnp.maximum(final_anchors, 0)], 0)
    column_of = final_ids // NBY
    along_y = final_ids % NBY
    position = (column_of - along_y) % columns * NBY + along_y
    result = by_position[position]
    return jnp.where((final_anchors >= 0)[:, None, None, None], result, jnp.zeros_like(result))
```

```python
import functools

import jax
import jax.numpy as jnp
from jax import lax
from jax.experimental import pallas as pl
from jax.experimental.pallas import tpu as pltpu
from jax.sharding import PartitionSpec as P

MESH = pl.DeviceIdType.MESH
BLK_MEAN = 6
OUT = 7
SEND = BLK_MEAN - 1
LANES = 128
DT = 0.12


def make_tables(slot_blocks, rows, cols, my_row, my_col):
    cap = slot_blocks.shape[1]
    levels = rows.bit_length() - 1
    half = rows // 2
    group = BLK_MEAN * rows
    ids = slot_blocks.reshape(rows, cols, cap)
    counts = jnp.sum((ids >= 0).astype(jnp.int32), axis=2)
    row_ids = jnp.arange(rows, dtype=jnp.int32)
    col_ids = jnp.arange(cols, dtype=jnp.int32)
    at_row = jnp.broadcast_to(row_ids[:, None, None], ids.shape)
    at_slot = jnp.broadcast_to(jnp.arange(cap, dtype=jnp.int32), ids.shape)
    mine = (row_ids[:, None] == my_row) & (col_ids[None, :] == my_col)
    scalars = []
    for level in range(levels):
        bit = 1 << level
        other = counts.reshape(rows // (2 * bit), 2, bit, cols)[:, ::-1].reshape(rows, cols)
        send = jnp.maximum(counts - other, 0) // 2
        take = jnp.maximum(other - counts, 0) // 2
        keep = counts - send
        scalars.append(jnp.sum(jnp.where(mine, keep, 0)))
        hit = at_row[None] == row_ids[:, None, None, None]
        keep_here = jnp.sum(jnp.where(hit, keep[:, None, :, None], 0), axis=0)
        other_here = jnp.sum(jnp.where(hit, other[:, None, :, None], 0), axis=0)
        moved = at_slot >= keep_here
        at_row = jnp.where(moved, at_row ^ bit, at_row)
        at_slot = jnp.where(moved, other_here + at_slot - keep_here, at_slot)
        counts = keep + take
    scalars.append(jnp.sum(jnp.where(mine, counts, 0)))
    place = at_row * 8 + at_slot
    flat_ids = ids.reshape(-1)
    flat_place = jnp.where(flat_ids >= 0, place.reshape(-1), 0)
    flat_col = jnp.broadcast_to(col_ids[None, :, None], ids.shape).reshape(-1)
    seats = jnp.stack([my_row, my_row ^ half])[:, None] * 8 + jnp.arange(OUT, dtype=jnp.int32)
    seats = seats.reshape(-1)
    match = (flat_place[None] == seats[:, None]) & (flat_col == my_col)[None] & (flat_ids >= 0)[None]
    along = jnp.sum(jnp.where(match, flat_ids[None] - my_col * group, 0), axis=1)
    below = ((my_col + cols - 1) % cols) * group
    above = ((my_col + 1) % cols) * group
    wanted = jnp.stack(
        [
            below + along,
            below + (along + group - 1) % group,
            above + along,
            above + (along + 1) % group,
        ]
    ).reshape(-1)
    found = jnp.sum(jnp.where(flat_ids[None] == wanted[:, None], flat_place[None], 0), axis=1)
    distance = (found // 8) ^ my_row
    source = distance * 8 + found % 8
    return jnp.concatenate([jnp.stack(scalars), source])


def cell_values(cons):
    rho, mx, my, mz, energy = cons
    inv = 1.0 / rho
    vel = (mx * inv, my * inv, mz * inv)
    p = 0.4 * (energy - 0.5 * rho * (vel[0] * vel[0] + vel[1] * vel[1] + vel[2] * vel[2]))
    theta = p * inv
    sound = jnp.sqrt(1.4 * theta)
    kappa = 0.2 * jnp.exp(0.7 * jnp.log(theta))
    return vel, p, theta, sound, kappa


def direction_values(cons, values, normal):
    vel, p, theta, sound, kappa = values
    un = vel[normal]
    flux = [cons[1 + normal], cons[1] * un, cons[2] * un, cons[3] * un, (cons[4] + p) * un]
    flux[1 + normal] = flux[1 + normal] + p
    return (*cons, *flux, jnp.abs(un) + sound, theta, kappa)


def face(low, high):
    half_speed = 0.5 * jnp.maximum(low[10], high[10])
    out = [0.5 * (low[5 + i] + high[5 + i]) - half_speed * (high[i] - low[i]) for i in range(5)]
    out[4] = out[4] - 0.5 * (low[12] + high[12]) * (high[11] - low[11])
    return out


def block_rate(cons, ghost_x, ghost_y):
    edge, flat = cons[0].shape
    row = lax.broadcasted_iota(jnp.int32, (edge, flat), 0)
    lane = lax.broadcasted_iota(jnp.int32, (edge, flat), 1)
    values = cell_values(cons)
    mid = direction_values(cons, values, 0)
    gx = direction_values(ghost_x, cell_values(ghost_x), 0)
    last = row == edge - 1
    up = [
        jnp.where(last, jnp.concatenate([g, g], axis=0), pltpu.roll(m, edge - 1, 0))
        for m, g in zip(mid, gx)
    ]
    upper = face(mid, up)
    bottom = face(gx, [m[:8] for m in mid])
    change = [
        u - jnp.where(row == 0, jnp.concatenate([b, b], axis=0), pltpu.roll(u, 1, 0))
        for u, b in zip(upper, bottom)
    ]
    mid = direction_values(cons, values, 1)
    gy = direction_values(ghost_y, cell_values(ghost_y), 1)
    last = lane >= flat - edge
    up = [
        jnp.where(last, jnp.concatenate([g, g], axis=1), pltpu.roll(m, flat - edge, 1))
        for m, g in zip(mid, gy)
    ]
    upper = face(mid, up)
    bottom = face(gy, [m[:, :LANES] for m in mid])
    change = [
        t + (u - jnp.where(lane < edge, jnp.concatenate([b, b], axis=1), pltpu.roll(u, edge, 1)))
        for t, u, b in zip(change, upper, bottom)
    ]
    mid = direction_values(cons, values, 2)
    up = [pltpu.roll(m, flat - 1, 1) for m in mid]
    upper = face(mid, up)
    height = lane % edge
    zero = jnp.zeros_like(values[1])
    wall = [zero, zero, zero, values[1], zero]
    change = [
        t
        + (
            jnp.where(height == edge - 1, w, u)
            - jnp.where(height == 0, w, pltpu.roll(u, 1, 1))
        )
        for t, u, w in zip(change, upper, wall)
    ]
    return [-t for t in change]


def kernel(rows, cols, cap, *refs):
    levels = rows.bit_length() - 1
    half = rows // 2
    refs = list(refs)
    tab, cells, out = refs[:3]
    refs = refs[3:]
    send_blocks = refs[:levels]
    recv_blocks = refs[levels : 2 * levels]
    refs = refs[2 * levels :]
    start, now = refs[:2]
    sections = [refs[2 + 8 * i : 10 + 8 * i] for i in range(3)]
    bsend, brecv, hsend, hrecv = refs[26:30]
    my_row, my_col = lax.axis_index("row"), lax.axis_index("col")
    left = (my_row, lax.rem(my_col + cols - 1, cols))
    right = (my_row, lax.rem(my_col + 1, cols))

    def partner(level):
        bit = 1 << level
        return (my_row + bit - 2 * bit * (lax.rem(my_row // bit, 2)), my_col)

    barrier = pltpu.get_barrier_semaphore()
    for device in [left, right] + [partner(level) for level in range(levels)]:
        pl.semaphore_signal(barrier, inc=1, device_id=device, device_id_type=MESH)
    pl.semaphore_wait(barrier, 2 + levels)

    def held(slot, depth):
        value = cells[jnp.minimum(slot, cap - 1)]
        for level in range(depth):
            keep = tab[level]
            got = recv_blocks[level][jnp.clip(slot - keep, 0, SEND - 1)]
            value = jnp.where(slot >= keep, got, value)
        return value

    for level in range(levels):
        for k in range(SEND):
            send_blocks[level][k] = held(tab[level] + k, level)
        copy = pltpu.make_async_remote_copy(
            src_ref=send_blocks[level],
            dst_ref=recv_blocks[level],
            send_sem=bsend.at[level],
            recv_sem=brecv.at[level],
            device_id=partner(level),
            device_id_type=MESH,
        )
        copy.start()
        copy.wait()

    def open_block(slot, carry):
        value = held(slot, levels)
        rho, u, v, w, p = (value[f] for f in range(5))
        energy = p / 0.4 + 0.5 * rho * (u * u + v * v + w * w)
        for f, field in enumerate((rho, rho * u, rho * v, rho * w, energy)):
            start[slot, f] = field
            now[slot, f] = field
        return carry

    lax.fori_loop(0, OUT, open_block, 0)

    edge = now.shape[2]
    tile_lane = lax.broadcasted_iota(jnp.int32, (edge, LANES), 1)
    ghost_row = lax.broadcasted_iota(jnp.int32, (8, 2 * LANES), 0)

    for step in range(3):
        hi_send, lo_send, lo_known, hi_known, lo_pick, hi_pick, lo_sel, hi_sel = sections[step]
        used = [0]

        def remote(src, dst, device):
            at = used[0]
            used[0] += 1
            copy = pltpu.make_async_remote_copy(
                src_ref=src,
                dst_ref=dst,
                send_sem=hsend.at[step, at],
                recv_sem=hrecv.at[step, at],
                device_id=device,
                device_id_type=MESH,
            )
            copy.start()
            return copy

        def pack(buffer, high):
            for f in range(5):
                tile = None
                for s in range(OUT):
                    if high:
                        piece = now[s, f, :, LANES : 2 * LANES]
                        shift = (edge * s + edge) % LANES
                    else:
                        piece = now[s, f, :, 0:LANES]
                        shift = edge * s
                    piece = pltpu.roll(piece, shift, 1) if shift else piece
                    tile = piece if tile is None else jnp.where(tile_lane // edge == s, piece, tile)
                    x = edge - 1 if high else 0
                    buffer[5 + f, s : s + 1, :] = now[s, f, x : x + 1, 0:LANES]
                    buffer[5 + f, 8 + s : 9 + s, :] = now[s, f, x : x + 1, LANES : 2 * LANES]
                buffer[f] = tile

        pack(hi_send, True)
        flights_lo = [remote(hi_send, lo_known.at[0], right)]
        pack(lo_send, False)
        flights_hi = [remote(lo_send, hi_known.at[0], left)]

        base = levels + 1

        def entry(kind, far, slot):
            return tab[base + (kind * 2 + far) * OUT + slot]

        def select(known, pick, first_kind):
            for s in range(OUT):
                code = entry(first_kind, 1, s)
                q, sigma = jnp.minimum(code // 8, half - 1), code % 8
                for f in range(5):
                    pick[5 + f, s : s + 1, :] = known[q, 5 + f, pl.ds(sigma, 1), :]
                    pick[5 + f, 8 + s : 9 + s, :] = known[q, 5 + f, pl.ds(8 + sigma, 1), :]
            shifts = []
            for s in range(OUT):
                code = entry(first_kind + 1, 1, s)
                q, sigma = jnp.minimum(code // 8, half - 1), code % 8
                shifts.append((q, lax.rem(edge * (s + 8 - sigma), LANES)))
            for f in range(5):
                tile = None
                for s, (q, shift) in enumerate(shifts):
                    piece = pltpu.roll(known[q, f], shift, 1)
                    tile = piece if tile is None else jnp.where(tile_lane // edge == s, piece, tile)
                pick[f] = tile

        for level in range(levels - 1):
            size = 1 << level
            for known, flights in ((lo_known, flights_lo), (hi_known, flights_hi)):
                flights[-1].wait()
                flights.append(
                    remote(known.at[pl.ds(0, size)], known.at[pl.ds(size, size)], partner(level))
                )
        for known, flights, pick, sel, kind in (
            (lo_known, flights_lo, lo_pick, lo_sel, 0),
            (hi_known, flights_hi, hi_pick, hi_sel, 2),
        ):
            flights[-1].wait()
            select(known, pick, kind)
            flights.append(remote(pick, sel, partner(levels - 1)))
        flights_lo[-1].wait()
        flights_hi[-1].wait()

        def advance(slot, carry):
            def place(kind):
                code = entry(kind, 0, slot)
                near = code < 8 * half
                q = jnp.minimum(code // 8, half - 1)
                return near, q, jnp.where(near, code % 8, slot)

            def x_row(known, sel, seat, f, top):
                near, q, sigma = seat
                a = known[q, 5 + f, pl.ds(top + sigma, 1), :]
                b = sel[5 + f, pl.ds(top + slot, 1), :]
                return jnp.where(near, a, b)

            def y_tile(known, sel, seat, f, to):
                near, q, sigma = seat
                tile = jnp.where(near, known[q, f], sel[f])
                return pltpu.roll(tile, lax.rem(LANES + to - edge * sigma, LANES), 1)

            x_lo, y_lo, x_hi, y_hi = (place(kind) for kind in range(4))
            ghost_x, ghost_y = [], []
            for f in range(5):
                low = jnp.concatenate(
                    [x_row(lo_known, lo_sel, x_lo, f, 0), x_row(lo_known, lo_sel, x_lo, f, 8)], axis=1
                )
                high = jnp.concatenate(
                    [x_row(hi_known, hi_sel, x_hi, f, 0), x_row(hi_known, hi_sel, x_hi, f, 8)], axis=1
                )
                ghost_x.append(jnp.where(ghost_row == 0, low, high))
                ghost_y.append(
                    jnp.where(
                        tile_lane < edge,
                        y_tile(lo_known, lo_sel, y_lo, f, 0),
                        y_tile(hi_known, hi_sel, y_hi, f, LANES - edge),
                    )
                )
            cons = tuple(now[slot, f] for f in range(5))
            rate = block_rate(cons, tuple(ghost_x), tuple(ghost_y))
            moved = [c + DT * d for c, d in zip(cons, rate)]
            if step == 1:
                moved = [0.75 * start[slot, f] + 0.25 * moved[f] for f in range(5)]
            if step == 2:
                moved = [(1.0 / 3.0) * start[slot, f] + (2.0 / 3.0) * moved[f] for f in range(5)]
                rho = moved[0]
                vel = [m / rho for m in moved[1:4]]
                p = 0.4 * (
                    moved[4] - 0.5 * rho * (vel[0] * vel[0] + vel[1] * vel[1] + vel[2] * vel[2])
                )
                filled = slot < tab[levels]
                for f, field in enumerate((rho, *vel, p)):
                    out[slot, f] = jnp.where(filled, field, 0.0)
            else:
                for f in range(5):
                    now[slot, f] = moved[f]
            return carry

        lax.fori_loop(0, OUT, advance, 0)


def body(rows, cols, block_cells, slot_blocks):
    cap = slot_blocks.shape[1]
    levels = rows.bit_length() - 1
    half = rows // 2
    edge, flat = block_cells.shape[2:]
    table = make_tables(slot_blocks, rows, cols, lax.axis_index("row"), lax.axis_index("col"))
    block = (5, edge, flat)
    faces = (10, 16, LANES)
    scratch = [pltpu.VMEM((SEND, *block), jnp.float32) for _ in range(2 * levels)]
    scratch += [pltpu.VMEM((OUT, *block), jnp.float32) for _ in range(2)]
    for _ in range(3):
        scratch += [pltpu.VMEM(faces, jnp.float32) for _ in range(2)]
        scratch += [pltpu.VMEM((half, *faces), jnp.float32) for _ in range(2)]
        scratch += [pltpu.VMEM(faces, jnp.float32) for _ in range(4)]
    scratch += [pltpu.SemaphoreType.DMA((levels,)) for _ in range(2)]
    scratch += [pltpu.SemaphoreType.DMA((3, 2 * (levels + 1))) for _ in range(2)]
    return pl.pallas_call(
        functools.partial(kernel, rows, cols, cap),
        out_shape=jax.ShapeDtypeStruct((OUT, *block), jnp.float32),
        in_specs=[
            pl.BlockSpec(memory_space=pltpu.SMEM),
            pl.BlockSpec(memory_space=pltpu.VMEM),
        ],
        out_specs=pl.BlockSpec(memory_space=pltpu.VMEM),
        scratch_shapes=scratch,
        compiler_params=pltpu.CompilerParams(
            collective_id=0, has_side_effects=True, vmem_limit_bytes=32 << 20
        ),
    )(table, block_cells)


def solution(mesh):
    rows, cols = mesh.shape["row"], mesh.shape["col"]
    return jax.shard_map(
        functools.partial(body, rows, cols),
        mesh=mesh,
        in_specs=(P(("row", "col"), None, None, None), P()),
        out_specs=P(("row", "col"), None, None, None),
        check_vma=False,
    )
```

```python
import functools

import jax
import jax.numpy as jnp
from jax import lax
from jax.experimental import pallas as pl
from jax.experimental.pallas import tpu as pltpu
from jax.sharding import PartitionSpec as P

MESH = pl.DeviceIdType.MESH
BLK_MEAN = 6
OUT = 7
SEND = BLK_MEAN - 1
LANES = 128
DT = 0.12


def make_tables(slot_blocks, rows, cols, my_row, my_col):
    cap = slot_blocks.shape[1]
    levels = rows.bit_length() - 1
    half = rows // 2
    group = BLK_MEAN * rows
    ids = slot_blocks.reshape(rows, cols, cap)
    counts = jnp.sum((ids >= 0).astype(jnp.int32), axis=2)
    row_ids = jnp.arange(rows, dtype=jnp.int32)
    col_ids = jnp.arange(cols, dtype=jnp.int32)
    at_row = jnp.broadcast_to(row_ids[:, None, None], ids.shape)
    at_slot = jnp.broadcast_to(jnp.arange(cap, dtype=jnp.int32), ids.shape)
    mine = (row_ids[:, None] == my_row) & (col_ids[None, :] == my_col)
    scalars = []
    for level in range(levels):
        bit = 1 << level
        other = counts.reshape(rows // (2 * bit), 2, bit, cols)[:, ::-1].reshape(rows, cols)
        send = jnp.maximum(counts - other, 0) // 2
        take = jnp.maximum(other - counts, 0) // 2
        keep = counts - send
        scalars.append(jnp.sum(jnp.where(mine, keep, 0)))
        hit = at_row[None] == row_ids[:, None, None, None]
        keep_here = jnp.sum(jnp.where(hit, keep[:, None, :, None], 0), axis=0)
        other_here = jnp.sum(jnp.where(hit, other[:, None, :, None], 0), axis=0)
        moved = at_slot >= keep_here
        at_row = jnp.where(moved, at_row ^ bit, at_row)
        at_slot = jnp.where(moved, other_here + at_slot - keep_here, at_slot)
        counts = keep + take
    scalars.append(jnp.sum(jnp.where(mine, counts, 0)))
    place = at_row * 16 + at_slot
    origin = row_ids[:, None, None] * 16 + jnp.arange(cap, dtype=jnp.int32)
    origin = jnp.broadcast_to(origin, ids.shape).reshape(-1)
    flat_ids = ids.reshape(-1)
    flat_place = jnp.where(flat_ids >= 0, place.reshape(-1), 0)
    flat_col = jnp.broadcast_to(col_ids[None, :, None], ids.shape).reshape(-1)
    seats = jnp.stack([my_row, my_row ^ half])[:, None] * 16 + jnp.arange(OUT, dtype=jnp.int32)
    seats = seats.reshape(-1)
    match = (flat_place[None] == seats[:, None]) & (flat_col == my_col)[None] & (flat_ids >= 0)[None]
    along = jnp.sum(jnp.where(match, flat_ids[None] - my_col * group, 0), axis=1)
    below = ((my_col + cols - 1) % cols) * group
    above = ((my_col + 1) % cols) * group
    wanted = jnp.stack(
        [
            below + along,
            below + (along + group - 1) % group,
            above + along,
            above + (along + 1) % group,
        ]
    ).reshape(-1)
    both = flat_place * 4096 + origin
    found = jnp.sum(jnp.where(flat_ids[None] == wanted[:, None], both[None], 0), axis=1)
    source = found ^ (my_row * 16 * 4097)
    source = jnp.concatenate([source % 4096, source // 4096])
    return jnp.concatenate([jnp.stack(scalars), source])


def cell_values(cons):
    rho, mx, my, mz, energy = cons
    inv = 1.0 / rho
    vel = (mx * inv, my * inv, mz * inv)
    p = 0.4 * (energy - 0.5 * rho * (vel[0] * vel[0] + vel[1] * vel[1] + vel[2] * vel[2]))
    theta = p * inv
    sound = jnp.sqrt(1.4 * theta)
    kappa = 0.2 * jnp.exp(0.7 * jnp.log(theta))
    return vel, p, theta, sound, kappa


def conserved(primitive):
    rho, u, v, w, p = primitive
    energy = p / 0.4 + 0.5 * rho * (u * u + v * v + w * w)
    return (rho, rho * u, rho * v, rho * w, energy)


def direction_values(cons, values, normal):
    vel, p, theta, sound, kappa = values
    un = vel[normal]
    flux = [cons[1 + normal], cons[1] * un, cons[2] * un, cons[3] * un, (cons[4] + p) * un]
    flux[1 + normal] = flux[1 + normal] + p
    return (*cons, *flux, jnp.abs(un) + sound, theta, kappa)


def face(low, high):
    half_speed = 0.5 * jnp.maximum(low[10], high[10])
    out = [0.5 * (low[5 + i] + high[5 + i]) - half_speed * (high[i] - low[i]) for i in range(5)]
    out[4] = out[4] - 0.5 * (low[12] + high[12]) * (high[11] - low[11])
    return out


def block_rate(cons, ghost_x, ghost_y):
    edge, flat = cons[0].shape
    row = lax.broadcasted_iota(jnp.int32, (edge, flat), 0)
    lane = lax.broadcasted_iota(jnp.int32, (edge, flat), 1)
    values = cell_values(cons)
    mid = direction_values(cons, values, 0)
    gx = direction_values(ghost_x, cell_values(ghost_x), 0)
    last = row == edge - 1
    up = [
        jnp.where(last, jnp.concatenate([g, g], axis=0), pltpu.roll(m, edge - 1, 0))
        for m, g in zip(mid, gx)
    ]
    upper = face(mid, up)
    bottom = face(gx, [m[:8] for m in mid])
    change = [
        u - jnp.where(row == 0, jnp.concatenate([b, b], axis=0), pltpu.roll(u, 1, 0))
        for u, b in zip(upper, bottom)
    ]
    mid = direction_values(cons, values, 1)
    gy = direction_values(ghost_y, cell_values(ghost_y), 1)
    last = lane >= flat - edge
    up = [
        jnp.where(last, jnp.concatenate([g, g], axis=1), pltpu.roll(m, flat - edge, 1))
        for m, g in zip(mid, gy)
    ]
    upper = face(mid, up)
    bottom = face(gy, [m[:, :LANES] for m in mid])
    change = [
        t + (u - jnp.where(lane < edge, jnp.concatenate([b, b], axis=1), pltpu.roll(u, edge, 1)))
        for t, u, b in zip(change, upper, bottom)
    ]
    mid = direction_values(cons, values, 2)
    up = [pltpu.roll(m, flat - 1, 1) for m in mid]
    upper = face(mid, up)
    height = lane % edge
    zero = jnp.zeros_like(values[1])
    wall = [zero, zero, zero, values[1], zero]
    change = [
        t
        + (
            jnp.where(height == edge - 1, w, u)
            - jnp.where(height == 0, w, pltpu.roll(u, 1, 1))
        )
        for t, u, w in zip(change, upper, wall)
    ]
    return [-t for t in change]


def y_units(n):
    return 2 * ((5 * n + 7) // 8)


def units(n):
    return y_units(n) + (10 * n + 7) // 8


def y_seat(slot, f):
    at = slot * 5 + f
    return 2 * (at // 8), 16 * (at % 8)


def x_seat(n, slot, f, part):
    at = slot * 10 + 2 * f + part
    return y_units(n) + at // 8, at % 8


def kernel(rows, cols, cap, *refs):
    levels = rows.bit_length() - 1
    half = rows // 2
    refs = list(refs)
    tab, cells, out = refs[:3]
    refs = refs[3:]
    send_blocks = refs[:levels]
    recv_blocks = refs[levels : 2 * levels]
    refs = refs[2 * levels :]
    start, now = refs[:2]
    sections = [refs[2 + 8 * i : 10 + 8 * i] for i in range(3)]
    bsend, brecv, hsend, hrecv = refs[26:30]
    my_row, my_col = lax.axis_index("row"), lax.axis_index("col")
    left = (my_row, lax.rem(my_col + cols - 1, cols))
    right = (my_row, lax.rem(my_col + 1, cols))

    def partner(level):
        bit = 1 << level
        return (my_row + bit - 2 * bit * (lax.rem(my_row // bit, 2)), my_col)

    barrier = pltpu.get_barrier_semaphore()
    for device in [left, right] + [partner(level) for level in range(levels)]:
        pl.semaphore_signal(barrier, inc=1, device_id=device, device_id_type=MESH)
    pl.semaphore_wait(barrier, 2 + levels)

    def held(slot, depth):
        value = cells[jnp.minimum(slot, cap - 1)]
        for level in range(depth):
            keep = tab[level]
            got = recv_blocks[level][jnp.clip(slot - keep, 0, SEND - 1)]
            value = jnp.where(slot >= keep, got, value)
        return value

    edge, flat = now.shape[2:]
    tile_lane = lax.broadcasted_iota(jnp.int32, (edge, LANES), 1)
    ghost_row = lax.broadcasted_iota(jnp.int32, (8, 2 * LANES), 0)

    def tile_of(ref, *seat):
        *lead, unit = seat
        return ref[(*lead, pl.ds(unit, 2))].reshape(edge, LANES)

    def put_tile(ref, unit, tile):
        ref[unit : unit + 2] = tile.reshape(2, 8, LANES)

    def move_blocks(level):
        for k in range(SEND):
            send_blocks[level][k] = held(tab[level] + k, level)
        copy = pltpu.make_async_remote_copy(
            src_ref=send_blocks[level],
            dst_ref=recv_blocks[level],
            send_sem=bsend.at[level],
            recv_sem=brecv.at[level],
            device_id=partner(level),
            device_id_type=MESH,
        )
        copy.start()
        return copy

    def remote(step, at, src, dst, device):
        copy = pltpu.make_async_remote_copy(
            src_ref=src,
            dst_ref=dst,
            send_sem=hsend.at[step, at],
            recv_sem=hrecv.at[step, at],
            device_id=device,
            device_id_type=MESH,
        )
        copy.start()
        return copy

    def pack(blocks, n, buffer, high):
        x = edge - 1 if high else 0
        side = slice(LANES, 2 * LANES) if high else slice(0, LANES)
        for first in range(0, 5 * n, 8):
            tile = None
            for at in range(first, min(first + 8, 5 * n)):
                s, f = at // 5, at % 5
                shift = (edge * (at - first) + (edge if high else 0)) % LANES
                piece = blocks[s, f, :, side]
                piece = pltpu.roll(piece, shift, 1) if shift else piece
                tile = piece if tile is None else jnp.where(tile_lane // edge == at - first, piece, tile)
            put_tile(buffer, 2 * (first // 8), tile)
        for s in range(n):
            for f in range(5):
                for part in range(2):
                    unit, row = x_seat(n, s, f, part)
                    buffer[unit, row : row + 1, :] = blocks[
                        s, f, x : x + 1, part * LANES : (part + 1) * LANES
                    ]

    base = levels + 1

    def entry(step, kind, far, slot):
        return tab[base + ((8 * OUT if step else 0) + (kind * 2 + far) * OUT + slot)]

    def near_seat(code):
        return jnp.minimum(code // 16, half - 1), code % 16

    def select(step, n, known, pick, first_kind):
        for s in range(OUT):
            q, sigma = near_seat(entry(step, first_kind, 1, s))
            for f in range(5):
                for part in range(2):
                    unit, row = x_seat(n, sigma, f, part)
                    to, at = x_seat(OUT, s, f, part)
                    pick[to, at : at + 1, :] = known[q, unit, pl.ds(row, 1), :]
        seats = [near_seat(entry(step, first_kind + 1, 1, s)) for s in range(OUT)]
        for first in range(0, 5 * OUT, 8):
            tile = None
            for at in range(first, min(first + 8, 5 * OUT)):
                q, sigma = seats[at // 5]
                unit, lane = y_seat(sigma, at % 5)
                shift = lax.rem(edge * (at - first) + LANES - lane, LANES)
                piece = pltpu.roll(tile_of(known, q, unit), shift, 1)
                tile = piece if tile is None else jnp.where(tile_lane // edge == at - first, piece, tile)
            put_tile(pick, 2 * (first // 8), tile)

    def begin(step, blocks, n):
        hi_send, lo_send, lo_known, hi_known = sections[step][:4]
        pack(blocks, n, hi_send, True)
        low = remote(step, 0, hi_send, lo_known.at[0], right)
        pack(blocks, n, lo_send, False)
        return [low, remote(step, 1, lo_send, hi_known.at[0], left)]

    def gather(step, flights):
        at = 2
        for level in range(levels - 1):
            size = 1 << level
            for side in range(2):
                known = sections[step][2 + side]
                flights[side].wait()
                flights[side] = remote(
                    step, at, known.at[pl.ds(0, size)], known.at[pl.ds(size, size)], partner(level)
                )
                at += 1
        return flights

    def trade(step, n, flights):
        for side in range(2):
            known, pick, sel = (sections[step][at + side] for at in (2, 4, 6))
            flights[side].wait()
            select(step, n, known, pick, 2 * side)
            flights[side] = remote(step, 2 * levels + side, pick, sel, partner(levels - 1))
        return flights

    def open_block(slot, carry):
        value = held(slot, levels)
        for f, field in enumerate(conserved([value[f] for f in range(5)])):
            start[slot, f] = field
            now[slot, f] = field
        return carry

    def advance(step, n):
        lo_known, hi_known, _, _, lo_sel, hi_sel = sections[step][2:]

        def run(slot, carry):
            def place(kind):
                code = entry(step, kind, 0, slot)
                return code < 16 * half, *near_seat(code)

            def x_row(known, sel, seat, f):
                near, q, sigma = seat
                parts = []
                for part in range(2):
                    unit, row = x_seat(n, sigma, f, part)
                    unit2, row2 = x_seat(OUT, slot, f, part)
                    a = known[q, unit, pl.ds(row, 1), :]
                    b = sel[unit2, pl.ds(row2, 1), :]
                    parts.append(jnp.where(near, a, b))
                return jnp.concatenate(parts, axis=1)

            def y_tile(known, sel, seat, f, to):
                near, q, sigma = seat
                unit, lane = y_seat(sigma, f)
                unit2, lane2 = y_seat(slot, f)
                tile = jnp.where(near, tile_of(known, q, unit), tile_of(sel, unit2))
                lane = jnp.where(near, lane, lane2)
                return pltpu.roll(tile, lax.rem(LANES + to - lane, LANES), 1)

            x_lo, y_lo, x_hi, y_hi = (place(kind) for kind in range(4))
            ghost_x, ghost_y = [], []
            for f in range(5):
                low = x_row(lo_known, lo_sel, x_lo, f)
                high = x_row(hi_known, hi_sel, x_hi, f)
                ghost_x.append(jnp.where(ghost_row == 0, low, high))
                low = y_tile(lo_known, lo_sel, y_lo, f, 0)
                high = y_tile(hi_known, hi_sel, y_hi, f, LANES - edge)
                ghost_y.append(jnp.where(tile_lane < edge, low, high))
            if step == 0:
                ghost_x, ghost_y = conserved(ghost_x), conserved(ghost_y)
            cons = tuple(now[slot, f] for f in range(5))
            rate = block_rate(cons, tuple(ghost_x), tuple(ghost_y))
            moved = [c + DT * d for c, d in zip(cons, rate)]
            if step == 1:
                moved = [0.75 * start[slot, f] + 0.25 * moved[f] for f in range(5)]
            if step == 2:
                moved = [(1.0 / 3.0) * start[slot, f] + (2.0 / 3.0) * moved[f] for f in range(5)]
                rho = moved[0]
                vel = [m / rho for m in moved[1:4]]
                p = 0.4 * (
                    moved[4] - 0.5 * rho * (vel[0] * vel[0] + vel[1] * vel[1] + vel[2] * vel[2])
                )
                filled = slot < tab[levels]
                for f, field in enumerate((rho, *vel, p)):
                    out[slot, f] = jnp.where(filled, field, 0.0)
            else:
                for f in range(5):
                    now[slot, f] = moved[f]
            return carry

        lax.fori_loop(0, OUT, run, 0)

    moving = move_blocks(0)
    flights = begin(0, cells, cap)
    flights = gather(0, flights)
    for level in range(1, levels):
        moving.wait()
        moving = move_blocks(level)
    flights = trade(0, cap, flights)
    moving.wait()
    lax.fori_loop(0, OUT, open_block, 0)
    for step in range(3):
        if step:
            flights = trade(step, OUT, gather(step, begin(step, now, OUT)))
        for flight in flights:
            flight.wait()
        advance(step, OUT if step else cap)


def body(rows, cols, block_cells, slot_blocks):
    cap = slot_blocks.shape[1]
    levels = rows.bit_length() - 1
    half = rows // 2
    edge, flat = block_cells.shape[2:]
    table = make_tables(slot_blocks, rows, cols, lax.axis_index("row"), lax.axis_index("col"))
    block = (5, edge, flat)
    scratch = [pltpu.VMEM((SEND, *block), jnp.float32) for _ in range(2 * levels)]
    scratch += [pltpu.VMEM((OUT, *block), jnp.float32) for _ in range(2)]
    for step in range(3):
        faces = (units(OUT if step else cap), 8, LANES)
        picked = (units(OUT), 8, LANES)
        scratch += [pltpu.VMEM(faces, jnp.float32) for _ in range(2)]
        scratch += [pltpu.VMEM((half, *faces), jnp.float32) for _ in range(2)]
        scratch += [pltpu.VMEM(picked, jnp.float32) for _ in range(4)]
    scratch += [pltpu.SemaphoreType.DMA((levels,)) for _ in range(2)]
    scratch += [pltpu.SemaphoreType.DMA((3, 2 * (levels + 1))) for _ in range(2)]
    return pl.pallas_call(
        functools.partial(kernel, rows, cols, cap),
        out_shape=jax.ShapeDtypeStruct((OUT, *block), jnp.float32),
        in_specs=[
            pl.BlockSpec(memory_space=pltpu.SMEM),
            pl.BlockSpec(memory_space=pltpu.VMEM),
        ],
        out_specs=pl.BlockSpec(memory_space=pltpu.VMEM),
        scratch_shapes=scratch,
        compiler_params=pltpu.CompilerParams(
            collective_id=0, has_side_effects=True, vmem_limit_bytes=32 << 20
        ),
    )(table, block_cells)


def solution(mesh):
    rows, cols = mesh.shape["row"], mesh.shape["col"]
    return jax.shard_map(
        functools.partial(body, rows, cols),
        mesh=mesh,
        in_specs=(P(("row", "col"), None, None, None), P()),
        out_specs=P(("row", "col"), None, None, None),
        check_vma=False,
    )
```

```python
import functools

import jax
import jax.numpy as jnp
from jax import lax
from jax.experimental import pallas as pl
from jax.experimental.pallas import tpu as pltpu
from jax.sharding import PartitionSpec as P

MESH = pl.DeviceIdType.MESH
BLK_MEAN = 6
OUT = 7
SEND = BLK_MEAN - 1
LANES = 128
DT = 0.12


def make_tables(slot_blocks, rows, cols, my_row, my_col):
    cap = slot_blocks.shape[1]
    levels = rows.bit_length() - 1
    half = rows // 2
    group = BLK_MEAN * rows
    ids = slot_blocks.reshape(rows, cols, cap)
    counts = jnp.sum((ids >= 0).astype(jnp.int32), axis=2)
    row_ids = jnp.arange(rows, dtype=jnp.int32)
    col_ids = jnp.arange(cols, dtype=jnp.int32)
    at_row = jnp.broadcast_to(row_ids[:, None, None], ids.shape)
    at_slot = jnp.broadcast_to(jnp.arange(cap, dtype=jnp.int32), ids.shape)
    mine = (row_ids[:, None] == my_row) & (col_ids[None, :] == my_col)
    scalars = []
    for level in range(levels):
        bit = 1 << level
        other = counts.reshape(rows // (2 * bit), 2, bit, cols)[:, ::-1].reshape(rows, cols)
        send = jnp.maximum(counts - other, 0) // 2
        take = jnp.maximum(other - counts, 0) // 2
        keep = counts - send
        scalars.append(jnp.sum(jnp.where(mine, keep, 0)))
        hit = at_row[None] == row_ids[:, None, None, None]
        keep_here = jnp.sum(jnp.where(hit, keep[:, None, :, None], 0), axis=0)
        other_here = jnp.sum(jnp.where(hit, other[:, None, :, None], 0), axis=0)
        moved = at_slot >= keep_here
        at_row = jnp.where(moved, at_row ^ bit, at_row)
        at_slot = jnp.where(moved, other_here + at_slot - keep_here, at_slot)
        counts = keep + take
    scalars.append(jnp.sum(jnp.where(mine, counts, 0)))
    place = at_row * 16 + at_slot
    origin = row_ids[:, None, None] * 16 + jnp.arange(cap, dtype=jnp.int32)
    origin = jnp.broadcast_to(origin, ids.shape).reshape(-1)
    flat_ids = ids.reshape(-1)
    flat_place = jnp.where(flat_ids >= 0, place.reshape(-1), 0)
    flat_col = jnp.broadcast_to(col_ids[None, :, None], ids.shape).reshape(-1)
    seats = jnp.stack([my_row, my_row ^ half])[:, None] * 16 + jnp.arange(OUT, dtype=jnp.int32)
    seats = seats.reshape(-1)
    match = (flat_place[None] == seats[:, None]) & (flat_col == my_col)[None] & (flat_ids >= 0)[None]
    along = jnp.sum(jnp.where(match, flat_ids[None] - my_col * group, 0), axis=1)
    below = ((my_col + cols - 1) % cols) * group
    above = ((my_col + 1) % cols) * group
    wanted = jnp.stack(
        [
            below + along,
            below + (along + group - 1) % group,
            above + along,
            above + (along + 1) % group,
        ]
    ).reshape(-1)
    both = flat_place * 4096 + origin
    found = jnp.sum(jnp.where(flat_ids[None] == wanted[:, None], both[None], 0), axis=1)
    source = found ^ (my_row * 16 * 4097)
    source = jnp.concatenate([source % 4096, source // 4096])
    return jnp.concatenate([jnp.stack(scalars), source])


def cell_values(cons):
    rho, mx, my, mz, energy = cons
    inv = 1.0 / rho
    vel = (mx * inv, my * inv, mz * inv)
    p = 0.4 * (energy - 0.5 * rho * (vel[0] * vel[0] + vel[1] * vel[1] + vel[2] * vel[2]))
    theta = p * inv
    sound = jnp.sqrt(1.4 * theta)
    kappa = 0.2 * jnp.exp(0.7 * jnp.log(theta))
    return vel, p, theta, sound, kappa


def conserved(primitive):
    rho, u, v, w, p = primitive
    energy = p / 0.4 + 0.5 * rho * (u * u + v * v + w * w)
    return (rho, rho * u, rho * v, rho * w, energy)


def direction_values(cons, values, normal):
    vel, p, theta, sound, kappa = values
    un = vel[normal]
    flux = [cons[1 + normal], cons[1] * un, cons[2] * un, cons[3] * un, (cons[4] + p) * un]
    flux[1 + normal] = flux[1 + normal] + p
    return (*cons, *flux, jnp.abs(un) + sound, theta, kappa)


def face(low, high):
    half_speed = 0.5 * jnp.maximum(low[10], high[10])
    out = [0.5 * (low[5 + i] + high[5 + i]) - half_speed * (high[i] - low[i]) for i in range(5)]
    out[4] = out[4] - 0.5 * (low[12] + high[12]) * (high[11] - low[11])
    return out


def block_rate(cons, ghost_x, ghost_y):
    edge, flat = cons[0].shape
    row = lax.broadcasted_iota(jnp.int32, (edge, flat), 0)
    lane = lax.broadcasted_iota(jnp.int32, (edge, flat), 1)
    values = cell_values(cons)
    mid = direction_values(cons, values, 0)
    gx = direction_values(ghost_x, cell_values(ghost_x), 0)
    last = row == edge - 1
    up = [
        jnp.where(last, jnp.concatenate([g, g], axis=0), pltpu.roll(m, edge - 1, 0))
        for m, g in zip(mid, gx)
    ]
    upper = face(mid, up)
    bottom = face(gx, [m[:8] for m in mid])
    change = [
        u - jnp.where(row == 0, jnp.concatenate([b, b], axis=0), pltpu.roll(u, 1, 0))
        for u, b in zip(upper, bottom)
    ]
    mid = direction_values(cons, values, 1)
    gy = direction_values(ghost_y, cell_values(ghost_y), 1)
    last = lane >= flat - edge
    up = [
        jnp.where(last, jnp.concatenate([g, g], axis=1), pltpu.roll(m, flat - edge, 1))
        for m, g in zip(mid, gy)
    ]
    upper = face(mid, up)
    bottom = face(gy, [m[:, :LANES] for m in mid])
    change = [
        t + (u - jnp.where(lane < edge, jnp.concatenate([b, b], axis=1), pltpu.roll(u, edge, 1)))
        for t, u, b in zip(change, upper, bottom)
    ]
    mid = direction_values(cons, values, 2)
    up = [pltpu.roll(m, flat - 1, 1) for m in mid]
    upper = face(mid, up)
    height = lane & (edge - 1)
    zero = jnp.zeros_like(values[1])
    wall = [zero, zero, zero, values[1], zero]
    change = [
        t
        + (
            jnp.where(height == edge - 1, w, u)
            - jnp.where(height == 0, w, pltpu.roll(u, 1, 1))
        )
        for t, u, w in zip(change, upper, wall)
    ]
    return [-t for t in change]


def y_units(n):
    return 2 * ((5 * n + 7) // 8)


def units(n):
    return y_units(n) + (10 * n + 7) // 8


def y_seat(slot, f):
    at = slot * 5 + f
    return 2 * (at >> 3), 16 * (at & 7)


def x_seat(n, slot, f, part):
    at = slot * 10 + 2 * f + part
    return y_units(n) + (at >> 3), at & 7


def kernel(rows, cols, cap, *refs):
    levels = rows.bit_length() - 1
    half = rows // 2
    refs = list(refs)
    tab, cells, out = refs[:3]
    refs = refs[3:]
    send_blocks = refs[:levels]
    recv_blocks = refs[levels : 2 * levels]
    refs = refs[2 * levels :]
    start, now = refs[:2]
    sections = [refs[2 + 8 * i : 10 + 8 * i] for i in range(3)]
    bsend, brecv, hsend, hrecv = refs[26:30]
    my_row, my_col = lax.axis_index("row"), lax.axis_index("col")
    left = (my_row, lax.rem(my_col + cols - 1, cols))
    right = (my_row, lax.rem(my_col + 1, cols))

    def partner(level):
        bit = 1 << level
        return (my_row + bit - 2 * bit * (lax.rem(my_row // bit, 2)), my_col)

    barrier = pltpu.get_barrier_semaphore()
    for device in [left, right] + [partner(level) for level in range(levels)]:
        pl.semaphore_signal(barrier, inc=1, device_id=device, device_id_type=MESH)
    pl.semaphore_wait(barrier, 2 + levels)

    def held(slot, depth):
        value = cells[jnp.minimum(slot, cap - 1)]
        for level in range(depth):
            keep = tab[level]
            got = recv_blocks[level][jnp.clip(slot - keep, 0, SEND - 1)]
            value = jnp.where(slot >= keep, got, value)
        return value

    edge, flat = now.shape[2:]
    tile_lane = lax.broadcasted_iota(jnp.int32, (edge, LANES), 1)
    tile_group = tile_lane >> 4
    ghost_row = lax.broadcasted_iota(jnp.int32, (8, 2 * LANES), 0)

    def tile_of(ref, *seat):
        *lead, unit = seat
        return ref[(*lead, pl.ds(unit, 2))].reshape(edge, LANES)

    def put_tile(ref, unit, tile):
        ref[unit : unit + 2] = tile.reshape(2, 8, LANES)

    def move_blocks(level):
        for k in range(SEND):
            send_blocks[level][k] = held(tab[level] + k, level)
        copy = pltpu.make_async_remote_copy(
            src_ref=send_blocks[level],
            dst_ref=recv_blocks[level],
            send_sem=bsend.at[level],
            recv_sem=brecv.at[level],
            device_id=partner(level),
            device_id_type=MESH,
        )
        copy.start()
        return copy

    def remote(step, at, src, dst, device):
        copy = pltpu.make_async_remote_copy(
            src_ref=src,
            dst_ref=dst,
            send_sem=hsend.at[step, at],
            recv_sem=hrecv.at[step, at],
            device_id=device,
            device_id_type=MESH,
        )
        copy.start()
        return copy

    def pack(blocks, n, buffer, high):
        x = edge - 1 if high else 0
        side = slice(LANES, 2 * LANES) if high else slice(0, LANES)
        for first in range(0, 5 * n, 8):
            tile = None
            for at in range(first, min(first + 8, 5 * n)):
                s, f = at // 5, at % 5
                shift = (edge * (at - first) + (edge if high else 0)) % LANES
                piece = blocks[s, f, :, side]
                piece = pltpu.roll(piece, shift, 1) if shift else piece
                tile = piece if tile is None else jnp.where(tile_group == at - first, piece, tile)
            put_tile(buffer, 2 * (first // 8), tile)
        for s in range(n):
            for f in range(5):
                for part in range(2):
                    unit, row = x_seat(n, s, f, part)
                    buffer[unit, row : row + 1, :] = blocks[
                        s, f, x : x + 1, part * LANES : (part + 1) * LANES
                    ]

    base = levels + 1

    def entry(step, kind, far, slot):
        return tab[base + ((8 * OUT if step else 0) + (kind * 2 + far) * OUT + slot)]

    def near_seat(code):
        return jnp.minimum(code >> 4, half - 1), code & 15

    def select(step, n, known, pick, first_kind):
        for s in range(OUT):
            q, sigma = near_seat(entry(step, first_kind, 1, s))
            for f in range(5):
                for part in range(2):
                    unit, row = x_seat(n, sigma, f, part)
                    to, at = x_seat(OUT, s, f, part)
                    pick[to, at : at + 1, :] = known[q, unit, pl.ds(row, 1), :]
        seats = [near_seat(entry(step, first_kind + 1, 1, s)) for s in range(OUT)]
        for first in range(0, 5 * OUT, 8):
            tile = None
            for at in range(first, min(first + 8, 5 * OUT)):
                q, sigma = seats[at // 5]
                unit, lane = y_seat(sigma, at % 5)
                shift = (edge * (at - first) + LANES - lane) & (LANES - 1)
                piece = pltpu.roll(tile_of(known, q, unit), shift, 1)
                tile = piece if tile is None else jnp.where(tile_group == at - first, piece, tile)
            put_tile(pick, 2 * (first // 8), tile)

    def begin(step, blocks, n):
        hi_send, lo_send, lo_known, hi_known = sections[step][:4]
        pack(blocks, n, hi_send, True)
        low = remote(step, 0, hi_send, lo_known.at[0], right)
        pack(blocks, n, lo_send, False)
        return [low, remote(step, 1, lo_send, hi_known.at[0], left)]

    def gather(step, flights):
        at = 2
        for level in range(levels - 1):
            size = 1 << level
            for side in range(2):
                known = sections[step][2 + side]
                flights[side].wait()
                flights[side] = remote(
                    step, at, known.at[pl.ds(0, size)], known.at[pl.ds(size, size)], partner(level)
                )
                at += 1
        return flights

    def trade(step, n, flights):
        for side in range(2):
            known, pick, sel = (sections[step][at + side] for at in (2, 4, 6))
            flights[side].wait()
            select(step, n, known, pick, 2 * side)
            flights[side] = remote(step, 2 * levels + side, pick, sel, partner(levels - 1))
        return flights

    def open_block(slot, carry):
        value = held(slot, levels)
        for f, field in enumerate(conserved([value[f] for f in range(5)])):
            start[slot, f] = field
            now[slot, f] = field
        return carry

    def advance(step, n):
        lo_known, hi_known, _, _, lo_sel, hi_sel = sections[step][2:]

        def run(slot, carry):
            def place(kind):
                code = entry(step, kind, 0, slot)
                return code < 16 * half, *near_seat(code)

            def x_row(known, sel, seat, f):
                near, q, sigma = seat
                parts = []
                for part in range(2):
                    unit, row = x_seat(n, sigma, f, part)
                    unit2, row2 = x_seat(OUT, slot, f, part)
                    a = known[q, unit, pl.ds(row, 1), :]
                    b = sel[unit2, pl.ds(row2, 1), :]
                    parts.append(jnp.where(near, a, b))
                return jnp.concatenate(parts, axis=1)

            def y_tile(known, sel, seat, f, to):
                near, q, sigma = seat
                unit, lane = y_seat(sigma, f)
                unit2, lane2 = y_seat(slot, f)
                tile = jnp.where(near, tile_of(known, q, unit), tile_of(sel, unit2))
                lane = jnp.where(near, lane, lane2)
                return pltpu.roll(tile, (LANES + to - lane) & (LANES - 1), 1)

            x_lo, y_lo, x_hi, y_hi = (place(kind) for kind in range(4))
            ghost_x, ghost_y = [], []
            for f in range(5):
                low = x_row(lo_known, lo_sel, x_lo, f)
                high = x_row(hi_known, hi_sel, x_hi, f)
                ghost_x.append(jnp.where(ghost_row == 0, low, high))
                low = y_tile(lo_known, lo_sel, y_lo, f, 0)
                high = y_tile(hi_known, hi_sel, y_hi, f, LANES - edge)
                ghost_y.append(jnp.where(tile_lane < edge, low, high))
            if step == 0:
                ghost_x, ghost_y = conserved(ghost_x), conserved(ghost_y)
            cons = tuple(now[slot, f] for f in range(5))
            rate = block_rate(cons, tuple(ghost_x), tuple(ghost_y))
            moved = [c + DT * d for c, d in zip(cons, rate)]
            if step == 1:
                moved = [0.75 * start[slot, f] + 0.25 * moved[f] for f in range(5)]
            if step == 2:
                moved = [(1.0 / 3.0) * start[slot, f] + (2.0 / 3.0) * moved[f] for f in range(5)]
                rho = moved[0]
                vel = [m / rho for m in moved[1:4]]
                p = 0.4 * (
                    moved[4] - 0.5 * rho * (vel[0] * vel[0] + vel[1] * vel[1] + vel[2] * vel[2])
                )
                filled = slot < tab[levels]
                for f, field in enumerate((rho, *vel, p)):
                    out[slot, f] = jnp.where(filled, field, 0.0)
            else:
                for f in range(5):
                    now[slot, f] = moved[f]
            return carry

        lax.fori_loop(0, OUT, run, 0)

    moving = move_blocks(0)
    flights = begin(0, cells, cap)
    flights = gather(0, flights)
    for level in range(1, levels):
        moving.wait()
        moving = move_blocks(level)
    flights = trade(0, cap, flights)
    moving.wait()
    lax.fori_loop(0, OUT, open_block, 0)
    for step in range(3):
        if step:
            flights = trade(step, OUT, gather(step, begin(step, now, OUT)))
        for flight in flights:
            flight.wait()
        advance(step, OUT if step else cap)


def body(rows, cols, block_cells, slot_blocks):
    cap = slot_blocks.shape[1]
    levels = rows.bit_length() - 1
    half = rows // 2
    edge, flat = block_cells.shape[2:]
    table = make_tables(slot_blocks, rows, cols, lax.axis_index("row"), lax.axis_index("col"))
    block = (5, edge, flat)
    scratch = [pltpu.VMEM((SEND, *block), jnp.float32) for _ in range(2 * levels)]
    scratch += [pltpu.VMEM((OUT, *block), jnp.float32) for _ in range(2)]
    for step in range(3):
        faces = (units(OUT if step else cap), 8, LANES)
        picked = (units(OUT), 8, LANES)
        scratch += [pltpu.VMEM(faces, jnp.float32) for _ in range(2)]
        scratch += [pltpu.VMEM((half, *faces), jnp.float32) for _ in range(2)]
        scratch += [pltpu.VMEM(picked, jnp.float32) for _ in range(4)]
    scratch += [pltpu.SemaphoreType.DMA((levels,)) for _ in range(2)]
    scratch += [pltpu.SemaphoreType.DMA((3, 2 * (levels + 1))) for _ in range(2)]
    return pl.pallas_call(
        functools.partial(kernel, rows, cols, cap),
        out_shape=jax.ShapeDtypeStruct((OUT, *block), jnp.float32),
        in_specs=[
            pl.BlockSpec(memory_space=pltpu.SMEM),
            pl.BlockSpec(memory_space=pltpu.VMEM),
        ],
        out_specs=pl.BlockSpec(memory_space=pltpu.VMEM),
        scratch_shapes=scratch,
        compiler_params=pltpu.CompilerParams(
            collective_id=0, has_side_effects=True, vmem_limit_bytes=32 << 20
        ),
    )(table, block_cells)


def solution(mesh):
    rows, cols = mesh.shape["row"], mesh.shape["col"]
    return jax.shard_map(
        functools.partial(body, rows, cols),
        mesh=mesh,
        in_specs=(P(("row", "col"), None, None, None), P()),
        out_specs=P(("row", "col"), None, None, None),
        check_vma=False,
    )
```

```python
import functools

import jax
import jax.numpy as jnp
from jax import lax
from jax.experimental import pallas as pl
from jax.experimental.pallas import tpu as pltpu
from jax.sharding import PartitionSpec as P

MESH = pl.DeviceIdType.MESH
BLK_MEAN = 6
OUT = 7
SEND = BLK_MEAN - 1
LANES = 128
DT = 0.12


def make_tables(slot_blocks, rows, cols, my_row, my_col):
    cap = slot_blocks.shape[1]
    levels = rows.bit_length() - 1
    half = rows // 2
    group = BLK_MEAN * rows
    ids = slot_blocks.reshape(rows, cols, cap)
    counts = jnp.sum((ids >= 0).astype(jnp.int32), axis=2)
    row_ids = jnp.arange(rows, dtype=jnp.int32)
    col_ids = jnp.arange(cols, dtype=jnp.int32)
    at_row = jnp.broadcast_to(row_ids[:, None, None], ids.shape)
    at_slot = jnp.broadcast_to(jnp.arange(cap, dtype=jnp.int32), ids.shape)
    mine = (row_ids[:, None] == my_row) & (col_ids[None, :] == my_col)
    scalars = []
    for level in range(levels):
        bit = 1 << level
        other = counts.reshape(rows // (2 * bit), 2, bit, cols)[:, ::-1].reshape(rows, cols)
        send = jnp.maximum(counts - other, 0) // 2
        take = jnp.maximum(other - counts, 0) // 2
        keep = counts - send
        scalars.append(jnp.sum(jnp.where(mine, keep, 0)))
        hit = at_row[None] == row_ids[:, None, None, None]
        keep_here = jnp.sum(jnp.where(hit, keep[:, None, :, None], 0), axis=0)
        other_here = jnp.sum(jnp.where(hit, other[:, None, :, None], 0), axis=0)
        moved = at_slot >= keep_here
        at_row = jnp.where(moved, at_row ^ bit, at_row)
        at_slot = jnp.where(moved, other_here + at_slot - keep_here, at_slot)
        counts = keep + take
    scalars.append(jnp.sum(jnp.where(mine, counts, 0)))
    place = at_row * 16 + at_slot
    origin = row_ids[:, None, None] * 16 + jnp.arange(cap, dtype=jnp.int32)
    origin = jnp.broadcast_to(origin, ids.shape).reshape(-1)
    flat_ids = ids.reshape(-1)
    flat_place = jnp.where(flat_ids >= 0, place.reshape(-1), 0)
    flat_col = jnp.broadcast_to(col_ids[None, :, None], ids.shape).reshape(-1)
    near_far = jnp.stack([my_row, my_row ^ half])
    left, right = (my_col + cols - 1) % cols, (my_col + 1) % cols
    seat_rows = jnp.concatenate([near_far[:1], near_far, near_far])
    seat_cols = jnp.stack([my_col, right, right, left, left])
    seats = (seat_rows[:, None] * 16 + jnp.arange(OUT, dtype=jnp.int32)).reshape(-1, 1)
    seat_cols = jnp.repeat(seat_cols, OUT)[:, None]
    match = (flat_place[None] == seats) & (flat_col[None] == seat_cols) & (flat_ids >= 0)[None]
    along = jnp.sum(jnp.where(match, flat_ids[None] - flat_col[None] * group, 0), axis=1)
    along = along.reshape(5, OUT)
    here, there_right, there_left = along[:1], along[1:3], along[3:5]
    down, up = (lambda a: (a + group - 1) % group), (lambda a: (a + 1) % group)
    mine = jnp.concatenate([left * group + here, left * group + down(here)])
    mine = jnp.concatenate([mine, right * group + here, right * group + up(here)])
    theirs = jnp.concatenate([there_right, down(there_right), there_left, up(there_left)])
    wanted = jnp.concatenate([mine, theirs + my_col * group]).reshape(-1)
    both = flat_place * 4096 + origin
    found = jnp.sum(jnp.where(flat_ids[None] == wanted[:, None], both[None], 0), axis=1)
    source = found ^ (my_row * 16 * 4097)
    source = jnp.concatenate([source & 4095, source >> 12])
    return jnp.concatenate([jnp.stack(scalars), source])


def cell_values(cons):
    rho, mx, my, mz, energy = cons
    inv = 1.0 / rho
    vel = (mx * inv, my * inv, mz * inv)
    p = 0.4 * (energy - 0.5 * rho * (vel[0] * vel[0] + vel[1] * vel[1] + vel[2] * vel[2]))
    theta = p * inv
    sound = jnp.sqrt(1.4 * theta)
    kappa = 0.2 * jnp.exp(0.7 * jnp.log(theta))
    return vel, p, theta, sound, kappa


def conserved(primitive):
    rho, u, v, w, p = primitive
    energy = p / 0.4 + 0.5 * rho * (u * u + v * v + w * w)
    return (rho, rho * u, rho * v, rho * w, energy)


def direction_values(cons, values, normal):
    vel, p, theta, sound, kappa = values
    un = vel[normal]
    flux = [cons[1 + normal], cons[1] * un, cons[2] * un, cons[3] * un, (cons[4] + p) * un]
    flux[1 + normal] = flux[1 + normal] + p
    return (*cons, *flux, jnp.abs(un) + sound, theta, kappa)


def face(low, high):
    half_speed = 0.5 * jnp.maximum(low[10], high[10])
    out = [0.5 * (low[5 + i] + high[5 + i]) - half_speed * (high[i] - low[i]) for i in range(5)]
    out[4] = out[4] - 0.5 * (low[12] + high[12]) * (high[11] - low[11])
    return out


def block_rate(cons, ghost_x, ghost_y):
    edge, flat = cons[0].shape
    row = lax.broadcasted_iota(jnp.int32, (edge, flat), 0)
    lane = lax.broadcasted_iota(jnp.int32, (edge, flat), 1)
    values = cell_values(cons)
    mid = direction_values(cons, values, 0)
    gx = direction_values(ghost_x, cell_values(ghost_x), 0)
    last = row == edge - 1
    up = [
        jnp.where(last, jnp.concatenate([g, g], axis=0), pltpu.roll(m, edge - 1, 0))
        for m, g in zip(mid, gx)
    ]
    upper = face(mid, up)
    bottom = face(gx, [m[:8] for m in mid])
    change = [
        u - jnp.where(row == 0, jnp.concatenate([b, b], axis=0), pltpu.roll(u, 1, 0))
        for u, b in zip(upper, bottom)
    ]
    mid = direction_values(cons, values, 1)
    gy = direction_values(ghost_y, cell_values(ghost_y), 1)
    last = lane >= flat - edge
    up = [
        jnp.where(last, jnp.concatenate([g, g], axis=1), pltpu.roll(m, flat - edge, 1))
        for m, g in zip(mid, gy)
    ]
    upper = face(mid, up)
    bottom = face(gy, [m[:, :LANES] for m in mid])
    change = [
        t + (u - jnp.where(lane < edge, jnp.concatenate([b, b], axis=1), pltpu.roll(u, edge, 1)))
        for t, u, b in zip(change, upper, bottom)
    ]
    mid = direction_values(cons, values, 2)
    up = [pltpu.roll(m, flat - 1, 1) for m in mid]
    upper = face(mid, up)
    height = lane & (edge - 1)
    zero = jnp.zeros_like(values[1])
    wall = [zero, zero, zero, values[1], zero]
    change = [
        t
        + (
            jnp.where(height == edge - 1, w, u)
            - jnp.where(height == 0, w, pltpu.roll(u, 1, 1))
        )
        for t, u, w in zip(change, upper, wall)
    ]
    return [-t for t in change]


def y_units(n):
    return 2 * ((5 * n + 7) // 8)


def units(n):
    return y_units(n) + (10 * n + 7) // 8


def y_seat(slot, f):
    at = slot * 5 + f
    return 2 * (at >> 3), 16 * (at & 7)


def x_seat(n, slot, f, part):
    at = slot * 10 + 2 * f + part
    return y_units(n) + (at >> 3), at & 7


def kernel(rows, cols, cap, *refs):
    levels = rows.bit_length() - 1
    half = rows // 2
    refs = list(refs)
    tab, cells, out = refs[:3]
    refs = refs[3:]
    send_blocks = refs[:levels]
    recv_blocks = refs[levels : 2 * levels]
    refs = refs[2 * levels :]
    start, now = refs[:2]
    sections = [refs[2 + 10 * i : 12 + 10 * i] for i in range(3)]
    bsend, brecv, hsend, hrecv = refs[32:36]
    my_row, my_col = lax.axis_index("row"), lax.axis_index("col")
    left = (my_row, lax.rem(my_col + cols - 1, cols))
    right = (my_row, lax.rem(my_col + 1, cols))

    def partner(level):
        bit = 1 << level
        return (my_row + bit - 2 * bit * (lax.rem(my_row // bit, 2)), my_col)

    barrier = pltpu.get_barrier_semaphore()
    across = partner(levels - 1)[0]
    beside = [(right, left), ((across, right[1]), (across, left[1]))]
    for device in [*beside[0], *beside[1]] + [partner(level) for level in range(levels)]:
        pl.semaphore_signal(barrier, inc=1, device_id=device, device_id_type=MESH)
    pl.semaphore_wait(barrier, 4 + levels)

    def held(slot, depth):
        value = cells[jnp.minimum(slot, cap - 1)]
        for level in range(depth):
            keep = tab[level]
            got = recv_blocks[level][jnp.clip(slot - keep, 0, SEND - 1)]
            value = jnp.where(slot >= keep, got, value)
        return value

    edge, flat = now.shape[2:]
    tile_lane = lax.broadcasted_iota(jnp.int32, (edge, LANES), 1)
    tile_group = tile_lane >> 4
    ghost_row = lax.broadcasted_iota(jnp.int32, (8, 2 * LANES), 0)

    def tile_of(ref, *seat):
        *lead, unit = seat
        return ref[(*lead, pl.ds(unit, 2))].reshape(edge, LANES)

    def put_tile(ref, unit, tile):
        ref[unit : unit + 2] = tile.reshape(2, 8, LANES)

    def move_blocks(level):
        for k in range(SEND):
            send_blocks[level][k] = held(tab[level] + k, level)
        copy = pltpu.make_async_remote_copy(
            src_ref=send_blocks[level],
            dst_ref=recv_blocks[level],
            send_sem=bsend.at[level],
            recv_sem=brecv.at[level],
            device_id=partner(level),
            device_id_type=MESH,
        )
        copy.start()
        return copy

    def remote(step, at, src, dst, device):
        copy = pltpu.make_async_remote_copy(
            src_ref=src,
            dst_ref=dst,
            send_sem=hsend.at[step, at],
            recv_sem=hrecv.at[step, at],
            device_id=device,
            device_id_type=MESH,
        )
        copy.start()
        return copy

    def pack(blocks, n, buffer, high):
        x = edge - 1 if high else 0
        side = slice(LANES, 2 * LANES) if high else slice(0, LANES)
        for first in range(0, 5 * n, 8):
            tile = None
            for at in range(first, min(first + 8, 5 * n)):
                s, f = at // 5, at % 5
                shift = (edge * (at - first) + (edge if high else 0)) % LANES
                piece = blocks[s, f, :, side]
                piece = pltpu.roll(piece, shift, 1) if shift else piece
                tile = piece if tile is None else jnp.where(tile_group == at - first, piece, tile)
            put_tile(buffer, 2 * (first // 8), tile)
        for s in range(n):
            for f in range(5):
                for part in range(2):
                    unit, row = x_seat(n, s, f, part)
                    buffer[unit, row : row + 1, :] = blocks[
                        s, f, x : x + 1, part * LANES : (part + 1) * LANES
                    ]

    base = levels + 1

    def entry(step, kind, far, slot):
        at = kind * OUT if far is None else 4 * OUT + (kind * 2 + far) * OUT
        return tab[base + (12 * OUT if step else 0) + at + slot]

    def near_seat(code):
        return jnp.minimum(code >> 4, half - 1), code & 15

    def select(step, n, known, pick, first_kind, far):
        for s in range(OUT):
            q, sigma = near_seat(entry(step, first_kind, far, s))
            for f in range(5):
                for part in range(2):
                    unit, row = x_seat(n, sigma, f, part)
                    to, at = x_seat(OUT, s, f, part)
                    pick[to, at : at + 1, :] = known[q, unit, pl.ds(row, 1), :]
        seats = [near_seat(entry(step, first_kind + 1, far, s)) for s in range(OUT)]
        for first in range(0, 5 * OUT, 8):
            tile = None
            for at in range(first, min(first + 8, 5 * OUT)):
                q, sigma = seats[at // 5]
                unit, lane = y_seat(sigma, at % 5)
                shift = (edge * (at - first) + LANES - lane) & (LANES - 1)
                piece = pltpu.roll(tile_of(known, q, unit), shift, 1)
                tile = piece if tile is None else jnp.where(tile_group == at - first, piece, tile)
            put_tile(pick, 2 * (first // 8), tile)

    def begin(step, blocks, n):
        flights = []
        for side in range(2):
            known = sections[step][side]
            pack(blocks, n, known.at[0], side == 0)
            if levels > 1:
                flights.append(remote(step, side, known.at[0], known.at[1], partner(0)))
        return flights

    def gather(step, flights):
        for level in range(1, levels - 1):
            size = 1 << level
            for side in range(2):
                known = sections[step][side]
                flights[side].wait()
                flights[side] = remote(
                    step,
                    2 * level + side,
                    known.at[pl.ds(0, size)],
                    known.at[pl.ds(size, size)],
                    partner(level),
                )
        return flights

    def trade(step, n, flights):
        sent = []
        for side in range(2):
            if flights:
                flights[side].wait()
            for far in (1, 0):
                known, pick, sel = (sections[step][at] for at in (side, 2 + 2 * side + far, 6 + 2 * side + far))
                select(step, n, known, pick, 2 * side, far)
                at = 2 * (levels - 1) + 2 * side + far
                sent.append(remote(step, at, pick, sel, beside[far][side]))
        return sent

    def open_block(slot, carry):
        value = held(slot, levels)
        for f, field in enumerate(conserved([value[f] for f in range(5)])):
            start[slot, f] = field
            now[slot, f] = field
        return carry

    def advance(step):
        lo_near, lo_far, hi_near, hi_far = sections[step][6:]

        def run(slot, carry):
            def near(kind):
                return entry(step, kind, None, slot) < 16 * half

            def x_row(close, away, kind, f):
                parts = []
                for part in range(2):
                    unit, row = x_seat(OUT, slot, f, part)
                    a = close[unit, pl.ds(row, 1), :]
                    b = away[unit, pl.ds(row, 1), :]
                    parts.append(jnp.where(near(kind), a, b))
                return jnp.concatenate(parts, axis=1)

            def y_tile(close, away, kind, f, to):
                unit, lane = y_seat(slot, f)
                tile = jnp.where(near(kind), tile_of(close, unit), tile_of(away, unit))
                return pltpu.roll(tile, (LANES + to - lane) & (LANES - 1), 1)

            ghost_x, ghost_y = [], []
            for f in range(5):
                low = x_row(lo_near, lo_far, 0, f)
                high = x_row(hi_near, hi_far, 2, f)
                ghost_x.append(jnp.where(ghost_row == 0, low, high))
                low = y_tile(lo_near, lo_far, 1, f, 0)
                high = y_tile(hi_near, hi_far, 3, f, LANES - edge)
                ghost_y.append(jnp.where(tile_lane < edge, low, high))
            if step == 0:
                ghost_x, ghost_y = conserved(ghost_x), conserved(ghost_y)
            cons = tuple(now[slot, f] for f in range(5))
            rate = block_rate(cons, tuple(ghost_x), tuple(ghost_y))
            moved = [c + DT * d for c, d in zip(cons, rate)]
            if step == 1:
                moved = [0.75 * start[slot, f] + 0.25 * moved[f] for f in range(5)]
            if step == 2:
                moved = [(1.0 / 3.0) * start[slot, f] + (2.0 / 3.0) * moved[f] for f in range(5)]
                rho = moved[0]
                vel = [m / rho for m in moved[1:4]]
                p = 0.4 * (
                    moved[4] - 0.5 * rho * (vel[0] * vel[0] + vel[1] * vel[1] + vel[2] * vel[2])
                )
                filled = slot < tab[levels]
                for f, field in enumerate((rho, *vel, p)):
                    out[slot, f] = jnp.where(filled, field, 0.0)
            else:
                for f in range(5):
                    now[slot, f] = moved[f]
            return carry

        lax.fori_loop(0, OUT, run, 0)

    moving = move_blocks(0)
    flights = begin(0, cells, cap)
    flights = gather(0, flights)
    for level in range(1, levels):
        moving.wait()
        moving = move_blocks(level)
    flights = trade(0, cap, flights)
    moving.wait()
    lax.fori_loop(0, OUT, open_block, 0)
    for step in range(3):
        if step:
            flights = trade(step, OUT, gather(step, begin(step, now, OUT)))
        for flight in flights:
            flight.wait()
        advance(step)


def body(rows, cols, block_cells, slot_blocks):
    cap = slot_blocks.shape[1]
    levels = rows.bit_length() - 1
    half = rows // 2
    edge, flat = block_cells.shape[2:]
    table = make_tables(slot_blocks, rows, cols, lax.axis_index("row"), lax.axis_index("col"))
    block = (5, edge, flat)
    scratch = [pltpu.VMEM((SEND, *block), jnp.float32) for _ in range(2 * levels)]
    scratch += [pltpu.VMEM((OUT, *block), jnp.float32) for _ in range(2)]
    for step in range(3):
        faces = (units(OUT if step else cap), 8, LANES)
        picked = (units(OUT), 8, LANES)
        scratch += [pltpu.VMEM((half, *faces), jnp.float32) for _ in range(2)]
        scratch += [pltpu.VMEM(picked, jnp.float32) for _ in range(8)]
    scratch += [pltpu.SemaphoreType.DMA((levels,)) for _ in range(2)]
    scratch += [pltpu.SemaphoreType.DMA((3, 2 * (levels + 1))) for _ in range(2)]
    return pl.pallas_call(
        functools.partial(kernel, rows, cols, cap),
        out_shape=jax.ShapeDtypeStruct((OUT, *block), jnp.float32),
        in_specs=[
            pl.BlockSpec(memory_space=pltpu.SMEM),
            pl.BlockSpec(memory_space=pltpu.VMEM),
        ],
        out_specs=pl.BlockSpec(memory_space=pltpu.VMEM),
        scratch_shapes=scratch,
        compiler_params=pltpu.CompilerParams(
            collective_id=0, has_side_effects=True, vmem_limit_bytes=32 << 20
        ),
    )(table, block_cells)


def solution(mesh):
    rows, cols = mesh.shape["row"], mesh.shape["col"]
    return jax.shard_map(
        functools.partial(body, rows, cols),
        mesh=mesh,
        in_specs=(P(("row", "col"), None, None, None), P()),
        out_specs=P(("row", "col"), None, None, None),
        check_vma=False,
    )
```

```python
import functools

import jax
import jax.numpy as jnp
from jax import lax
from jax.experimental import pallas as pl
from jax.experimental.pallas import tpu as pltpu
from jax.sharding import PartitionSpec as P

MESH = pl.DeviceIdType.MESH
BLK_MEAN = 6
OUT = 7
SEND = BLK_MEAN - 1
LANES = 128
DT = 0.12


def make_tables(slot_blocks, rows, cols, my_row, my_col):
    cap = slot_blocks.shape[1]
    levels = rows.bit_length() - 1
    half = rows // 2
    group = BLK_MEAN * rows
    ids = slot_blocks.reshape(rows, cols, cap)
    counts = jnp.sum((ids >= 0).astype(jnp.int32), axis=2)
    row_ids = jnp.arange(rows, dtype=jnp.int32)
    col_ids = jnp.arange(cols, dtype=jnp.int32)
    at_row = jnp.broadcast_to(row_ids[:, None, None], ids.shape)
    at_slot = jnp.broadcast_to(jnp.arange(cap, dtype=jnp.int32), ids.shape)
    mine = (row_ids[:, None] == my_row) & (col_ids[None, :] == my_col)
    scalars = []
    for level in range(levels):
        bit = 1 << level
        other = counts.reshape(rows // (2 * bit), 2, bit, cols)[:, ::-1].reshape(rows, cols)
        send = jnp.maximum(counts - other, 0) // 2
        take = jnp.maximum(other - counts, 0) // 2
        keep = counts - send
        scalars.append(jnp.sum(jnp.where(mine, keep, 0)))
        hit = at_row[None] == row_ids[:, None, None, None]
        keep_here = jnp.sum(jnp.where(hit, keep[:, None, :, None], 0), axis=0)
        other_here = jnp.sum(jnp.where(hit, other[:, None, :, None], 0), axis=0)
        moved = at_slot >= keep_here
        at_row = jnp.where(moved, at_row ^ bit, at_row)
        at_slot = jnp.where(moved, other_here + at_slot - keep_here, at_slot)
        counts = keep + take
    scalars.append(jnp.sum(jnp.where(mine, counts, 0)))
    place = at_row * 16 + at_slot
    origin = row_ids[:, None, None] * 16 + jnp.arange(cap, dtype=jnp.int32)
    origin = jnp.broadcast_to(origin, ids.shape).reshape(-1)
    flat_ids = ids.reshape(-1)
    flat_place = jnp.where(flat_ids >= 0, place.reshape(-1), 0)
    flat_col = jnp.broadcast_to(col_ids[None, :, None], ids.shape).reshape(-1)
    near_far = jnp.stack([my_row, my_row ^ half])
    left, right = (my_col + cols - 1) % cols, (my_col + 1) % cols
    seat_rows = jnp.concatenate([near_far[:1], near_far, near_far])
    seat_cols = jnp.stack([my_col, right, right, left, left])
    seats = (seat_rows[:, None] * 16 + jnp.arange(OUT, dtype=jnp.int32)).reshape(-1, 1)
    seat_cols = jnp.repeat(seat_cols, OUT)[:, None]
    match = (flat_place[None] == seats) & (flat_col[None] == seat_cols) & (flat_ids >= 0)[None]
    along = jnp.sum(jnp.where(match, flat_ids[None] - flat_col[None] * group, 0), axis=1)
    along = along.reshape(5, OUT)
    here, there_right, there_left = along[:1], along[1:3], along[3:5]
    down, up = (lambda a: (a + group - 1) % group), (lambda a: (a + 1) % group)
    mine = jnp.concatenate([left * group + here, left * group + down(here)])
    mine = jnp.concatenate([mine, right * group + here, right * group + up(here)])
    theirs = jnp.concatenate([there_right, down(there_right), there_left, up(there_left)])
    wanted = jnp.concatenate([mine, theirs + my_col * group]).reshape(-1)
    both = flat_place * 4096 + origin
    found = jnp.sum(jnp.where(flat_ids[None] == wanted[:, None], both[None], 0), axis=1)
    source = found ^ (my_row * 16 * 4097)
    source = jnp.concatenate([source & 4095, source >> 12])
    return jnp.concatenate([jnp.stack(scalars), source])


def cell_values(cons):
    rho, mx, my, mz, energy = cons
    inv = 1.0 / rho
    vel = (mx * inv, my * inv, mz * inv)
    p = 0.4 * (energy - 0.5 * rho * (vel[0] * vel[0] + vel[1] * vel[1] + vel[2] * vel[2]))
    theta = p * inv
    sound = jnp.sqrt(1.4 * theta)
    kappa = 0.2 * jnp.exp(0.7 * jnp.log(theta))
    return vel, p, theta, sound, kappa


def conserved(primitive):
    rho, u, v, w, p = primitive
    energy = p / 0.4 + 0.5 * rho * (u * u + v * v + w * w)
    return (rho, rho * u, rho * v, rho * w, energy)


def direction_values(cons, values, normal):
    vel, p, theta, sound, kappa = values
    un = vel[normal]
    flux = [cons[1 + normal], cons[1] * un, cons[2] * un, cons[3] * un, (cons[4] + p) * un]
    flux[1 + normal] = flux[1 + normal] + p
    return (*cons, *flux, jnp.abs(un) + sound, theta, kappa)


def face(low, high):
    half_speed = 0.5 * jnp.maximum(low[10], high[10])
    out = [0.5 * (low[5 + i] + high[5 + i]) - half_speed * (high[i] - low[i]) for i in range(5)]
    out[4] = out[4] - 0.5 * (low[12] + high[12]) * (high[11] - low[11])
    return out


def block_rate(cons, ghost_x, ghost_y):
    edge, flat = cons[0].shape
    row = lax.broadcasted_iota(jnp.int32, (edge, flat), 0)
    lane = lax.broadcasted_iota(jnp.int32, (edge, flat), 1)
    values = cell_values(cons)
    mid = direction_values(cons, values, 0)
    gx = direction_values(ghost_x, cell_values(ghost_x), 0)
    last = row == edge - 1
    up = [
        jnp.where(last, jnp.concatenate([g, g], axis=0), pltpu.roll(m, edge - 1, 0))
        for m, g in zip(mid, gx)
    ]
    upper = face(mid, up)
    bottom = face(gx, [m[:8] for m in mid])
    change = [
        u - jnp.where(row == 0, jnp.concatenate([b, b], axis=0), pltpu.roll(u, 1, 0))
        for u, b in zip(upper, bottom)
    ]
    mid = direction_values(cons, values, 1)
    gy = direction_values(ghost_y, cell_values(ghost_y), 1)
    last = lane >= flat - edge
    up = [
        jnp.where(last, jnp.concatenate([g, g], axis=1), pltpu.roll(m, flat - edge, 1))
        for m, g in zip(mid, gy)
    ]
    upper = face(mid, up)
    bottom = face(gy, [m[:, :LANES] for m in mid])
    change = [
        t + (u - jnp.where(lane < edge, jnp.concatenate([b, b], axis=1), pltpu.roll(u, edge, 1)))
        for t, u, b in zip(change, upper, bottom)
    ]
    mid = direction_values(cons, values, 2)
    up = [pltpu.roll(m, flat - 1, 1) for m in mid]
    upper = face(mid, up)
    height = lane & (edge - 1)
    zero = jnp.zeros_like(values[1])
    wall = [zero, zero, zero, values[1], zero]
    change = [
        t
        + (
            jnp.where(height == edge - 1, w, u)
            - jnp.where(height == 0, w, pltpu.roll(u, 1, 1))
        )
        for t, u, w in zip(change, upper, wall)
    ]
    return [-t for t in change]


def y_units(n):
    return 2 * ((5 * n + 7) // 8)


def units(n):
    return y_units(n) + (10 * n + 7) // 8


def y_seat(slot, f):
    at = slot * 5 + f
    return 2 * (at >> 3), 16 * (at & 7)


def x_seat(n, slot, f, part):
    at = slot * 10 + 2 * f + part
    return y_units(n) + (at >> 3), at & 7


def kernel(rows, cols, cap, *refs):
    levels = rows.bit_length() - 1
    half = rows // 2
    refs = list(refs)
    tab, cells, out = refs[:3]
    refs = refs[3:]
    send_blocks = refs[:levels]
    recv_blocks = refs[levels : 2 * levels]
    refs = refs[2 * levels :]
    start, now = refs[:2]
    sections = [refs[2 + 10 * i : 12 + 10 * i] for i in range(3)]
    bsend, brecv, hsend, hrecv = refs[32:36]
    my_row, my_col = lax.axis_index("row"), lax.axis_index("col")
    left = (my_row, lax.rem(my_col + cols - 1, cols))
    right = (my_row, lax.rem(my_col + 1, cols))

    def partner(level):
        bit = 1 << level
        return (my_row + bit - 2 * bit * (lax.rem(my_row // bit, 2)), my_col)

    barrier = pltpu.get_barrier_semaphore()
    across = partner(levels - 1)[0]
    beside = [(right, left), ((across, right[1]), (across, left[1]))]
    for device in [*beside[0], *beside[1]] + [partner(level) for level in range(levels)]:
        pl.semaphore_signal(barrier, inc=1, device_id=device, device_id_type=MESH)
    pl.semaphore_wait(barrier, 4 + levels)

    def held(slot, depth):
        value = cells[jnp.minimum(slot, cap - 1)]
        for level in range(depth):
            keep = tab[level]
            got = recv_blocks[level][jnp.clip(slot - keep, 0, SEND - 1)]
            value = jnp.where(slot >= keep, got, value)
        return value

    edge, flat = now.shape[2:]
    tile_lane = lax.broadcasted_iota(jnp.int32, (edge, LANES), 1)
    tile_group = tile_lane >> 4
    ghost_row = lax.broadcasted_iota(jnp.int32, (8, 2 * LANES), 0)

    def tile_of(ref, *seat):
        *lead, unit = seat
        return ref[(*lead, pl.ds(unit, 2))].reshape(edge, LANES)

    def put_tile(ref, unit, tile):
        ref[unit : unit + 2] = tile.reshape(2, 8, LANES)

    def move_blocks(level):
        for k in range(SEND):
            send_blocks[level][k] = held(tab[level] + k, level)
        copy = pltpu.make_async_remote_copy(
            src_ref=send_blocks[level],
            dst_ref=recv_blocks[level],
            send_sem=bsend.at[level],
            recv_sem=brecv.at[level],
            device_id=partner(level),
            device_id_type=MESH,
        )
        copy.start()
        return copy

    def remote(step, at, src, dst, device):
        copy = pltpu.make_async_remote_copy(
            src_ref=src,
            dst_ref=dst,
            send_sem=hsend.at[step, at],
            recv_sem=hrecv.at[step, at],
            device_id=device,
            device_id_type=MESH,
        )
        copy.start()
        return copy

    def pack(blocks, n, buffer, high):
        x = edge - 1 if high else 0
        side = slice(LANES, 2 * LANES) if high else slice(0, LANES)
        for first in range(0, 5 * n, 8):
            tile = None
            for at in range(first, min(first + 8, 5 * n)):
                s, f = at // 5, at % 5
                shift = (edge * (at - first) + (edge if high else 0)) % LANES
                piece = blocks[s, f, :, side]
                piece = pltpu.roll(piece, shift, 1) if shift else piece
                tile = piece if tile is None else jnp.where(tile_group == at - first, piece, tile)
            put_tile(buffer, 2 * (first // 8), tile)
        for s in range(n):
            for f in range(5):
                for part in range(2):
                    unit, row = x_seat(n, s, f, part)
                    buffer[unit, row : row + 1, :] = blocks[
                        s, f, x : x + 1, part * LANES : (part + 1) * LANES
                    ]

    base = levels + 1

    def entry(step, kind, far, slot):
        at = kind * OUT if far is None else 4 * OUT + (kind * 2 + far) * OUT
        return tab[base + (12 * OUT if step else 0) + at + slot]

    def near_seat(code):
        return jnp.minimum(code >> 4, half - 1), code & 15

    def select(step, n, known, pick, first_kind, far):
        for s in range(OUT):
            q, sigma = near_seat(entry(step, first_kind, far, s))
            for f in range(5):
                for part in range(2):
                    unit, row = x_seat(n, sigma, f, part)
                    to, at = x_seat(OUT, s, f, part)
                    pick[to, at : at + 1, :] = known[q, unit, pl.ds(row, 1), :]
        seats = [near_seat(entry(step, first_kind + 1, far, s)) for s in range(OUT)]
        for first in range(0, 5 * OUT, 8):
            tile = None
            for at in range(first, min(first + 8, 5 * OUT)):
                q, sigma = seats[at // 5]
                unit, lane = y_seat(sigma, at % 5)
                shift = (edge * (at - first) + LANES - lane) & (LANES - 1)
                piece = pltpu.roll(tile_of(known, q, unit), shift, 1)
                tile = piece if tile is None else jnp.where(tile_group == at - first, piece, tile)
            put_tile(pick, 2 * (first // 8), tile)

    def begin(step, blocks, n):
        flights = []
        for side in range(2):
            known = sections[step][side]
            pack(blocks, n, known.at[0], side == 0)
            if levels > 1:
                flights.append(remote(step, side, known.at[0], known.at[1], partner(0)))
        return flights

    def gather(step, flights):
        for level in range(1, levels - 1):
            size = 1 << level
            for side in range(2):
                known = sections[step][side]
                flights[side].wait()
                flights[side] = remote(
                    step,
                    2 * level + side,
                    known.at[pl.ds(0, size)],
                    known.at[pl.ds(size, size)],
                    partner(level),
                )
        return flights

    def trade(step, n, flights):
        sent = []
        for far in (1, 0):
            for side in range(2):
                if flights and far:
                    flights[side].wait()
                known, pick, sel = (sections[step][at] for at in (side, 2 + 2 * side + far, 6 + 2 * side + far))
                select(step, n, known, pick, 2 * side, far)
                at = 2 * (levels - 1) + 2 * side + far
                sent.append(remote(step, at, pick, sel, beside[far][side]))
        return sent

    def open_block(slot, carry):
        value = held(slot, levels)
        for f, field in enumerate(conserved([value[f] for f in range(5)])):
            start[slot, f] = field
            now[slot, f] = field
        return carry

    def advance(step):
        lo_near, lo_far, hi_near, hi_far = sections[step][6:]

        def run(slot, carry):
            def near(kind):
                return entry(step, kind, None, slot) < 16 * half

            def x_row(close, away, kind, f):
                parts = []
                for part in range(2):
                    unit, row = x_seat(OUT, slot, f, part)
                    a = close[unit, pl.ds(row, 1), :]
                    b = away[unit, pl.ds(row, 1), :]
                    parts.append(jnp.where(near(kind), a, b))
                return jnp.concatenate(parts, axis=1)

            def y_tile(close, away, kind, f, to):
                unit, lane = y_seat(slot, f)
                tile = jnp.where(near(kind), tile_of(close, unit), tile_of(away, unit))
                return pltpu.roll(tile, (LANES + to - lane) & (LANES - 1), 1)

            ghost_x, ghost_y = [], []
            for f in range(5):
                low = x_row(lo_near, lo_far, 0, f)
                high = x_row(hi_near, hi_far, 2, f)
                ghost_x.append(jnp.where(ghost_row == 0, low, high))
                low = y_tile(lo_near, lo_far, 1, f, 0)
                high = y_tile(hi_near, hi_far, 3, f, LANES - edge)
                ghost_y.append(jnp.where(tile_lane < edge, low, high))
            if step == 0:
                ghost_x, ghost_y = conserved(ghost_x), conserved(ghost_y)
            cons = tuple(now[slot, f] for f in range(5))
            rate = block_rate(cons, tuple(ghost_x), tuple(ghost_y))
            moved = [c + DT * d for c, d in zip(cons, rate)]
            if step == 1:
                moved = [0.75 * start[slot, f] + 0.25 * moved[f] for f in range(5)]
            if step == 2:
                moved = [(1.0 / 3.0) * start[slot, f] + (2.0 / 3.0) * moved[f] for f in range(5)]
                rho = moved[0]
                vel = [m / rho for m in moved[1:4]]
                p = 0.4 * (
                    moved[4] - 0.5 * rho * (vel[0] * vel[0] + vel[1] * vel[1] + vel[2] * vel[2])
                )
                filled = slot < tab[levels]
                for f, field in enumerate((rho, *vel, p)):
                    out[slot, f] = jnp.where(filled, field, 0.0)
            else:
                for f in range(5):
                    now[slot, f] = moved[f]
            return carry

        lax.fori_loop(0, OUT, run, 0)

    moving = move_blocks(0)
    flights = begin(0, cells, cap)
    flights = gather(0, flights)
    for level in range(1, levels):
        moving.wait()
        moving = move_blocks(level)
    flights = trade(0, cap, flights)
    moving.wait()
    lax.fori_loop(0, OUT, open_block, 0)
    for step in range(3):
        if step:
            flights = trade(step, OUT, gather(step, begin(step, now, OUT)))
        for flight in flights:
            flight.wait()
        advance(step)


def body(rows, cols, block_cells, slot_blocks):
    cap = slot_blocks.shape[1]
    levels = rows.bit_length() - 1
    half = rows // 2
    edge, flat = block_cells.shape[2:]
    table = make_tables(slot_blocks, rows, cols, lax.axis_index("row"), lax.axis_index("col"))
    block = (5, edge, flat)
    scratch = [pltpu.VMEM((SEND, *block), jnp.float32) for _ in range(2 * levels)]
    scratch += [pltpu.VMEM((OUT, *block), jnp.float32) for _ in range(2)]
    for step in range(3):
        faces = (units(OUT if step else cap), 8, LANES)
        picked = (units(OUT), 8, LANES)
        scratch += [pltpu.VMEM((half, *faces), jnp.float32) for _ in range(2)]
        scratch += [pltpu.VMEM(picked, jnp.float32) for _ in range(8)]
    scratch += [pltpu.SemaphoreType.DMA((levels,)) for _ in range(2)]
    scratch += [pltpu.SemaphoreType.DMA((3, 2 * (levels + 1))) for _ in range(2)]
    return pl.pallas_call(
        functools.partial(kernel, rows, cols, cap),
        out_shape=jax.ShapeDtypeStruct((OUT, *block), jnp.float32),
        in_specs=[
            pl.BlockSpec(memory_space=pltpu.SMEM),
            pl.BlockSpec(memory_space=pltpu.VMEM),
        ],
        out_specs=pl.BlockSpec(memory_space=pltpu.VMEM),
        scratch_shapes=scratch,
        compiler_params=pltpu.CompilerParams(
            collective_id=0, has_side_effects=True, vmem_limit_bytes=32 << 20
        ),
    )(table, block_cells)


def solution(mesh):
    rows, cols = mesh.shape["row"], mesh.shape["col"]
    return jax.shard_map(
        functools.partial(body, rows, cols),
        mesh=mesh,
        in_specs=(P(("row", "col"), None, None, None), P()),
        out_specs=P(("row", "col"), None, None, None),
        check_vma=False,
    )
```
